256 devices in a mesh: ctx: 64 (over z, x, core), head: 4 (over y).
Axes of the slice: x: 4, y: 4, z: 8, core: 2. Of those that a mesh axis runs over, the one named last changes fastest.
Arguments:
- mixer_input: bfloat16 [2, 4096, 16384], P(None, ('ctx', 'head')), may hold values from -6 to 6
- gate_input: bfloat16 [2, 4096, 16384], P(None, ('ctx', 'head')), may hold values from -6 to 6
- step_input: bfloat16 [2, 4096, 16384], P(None, ('ctx', 'head'))
- state_proj: bfloat16 [2, 4096, 32], P(None, 'ctx'), may hold values from -4 to 4
- conv_weight: bfloat16 [4, 16384], replicated, may hold values from -3 to 3
- conv_bias: float32 [16384], replicated, may hold values from -1 to 1
- step_bias: float32 [16384], P('head')
- decay_log: float32 [16, 16384], P(None, 'head'), may hold values from -0.7 to 0.7
- skip_gain: float32 [16384], P('head'), may hold values from 0.5 to 1.5
- query_states: bfloat16 [2, 4096, 8192], P(None, ('ctx', 'head')), may hold values from -5 to 5
- key_states: bfloat16 [2, 4096, 1024], P(None, ('ctx', 'head')), may hold values from -5 to 5
- value_states: bfloat16 [2, 4096, 1024], P(None, ('ctx', 'head')), may hold values from -6 to 6
- lengths: int32 [2], replicated, may hold values from 1024 to 4096, as said below
Outputs:
- mixer_output: bfloat16 [2, 4096, 16384], P(None, 'ctx', 'head')
- attention_output: bfloat16 [2, 4096, 8192], P(None, 'ctx', 'head')
The draws below stay inside these ranges and needn't reach their ends.
Inputs may be any that keep to these rules, and one draw needn't show every extreme that they name: `lengths`: one of the 2 sequences has length 4096.
All inputs are finite; a program needn't handle non-finite values.
Results may differ from the reference program's by a relative error of at most 0.0043.
Values may be sent and summed in bfloat16 or wider, within the bound.
No kernel may reach another device: no remote copies, remote signals or barrier semaphores. Data moves between devices by JAX's collectives and lax.ppermute only.
A program may use at most 256 MiB of HBM per device.

```python
import math
import jax
import jax.numpy as jnp
from jax import lax

DI = 16384
DSTATE = 16
CONV = 4
QH = 64
KVH = 8
HD = 128
SEQUENCE_COUNT = 2
SEQUENCE_LENGTH = 4096


def draw_query_states(key, part):
    array_shape = (SEQUENCE_COUNT, SEQUENCE_LENGTH, QH * HD)
    drawn_values = jnp.clip(jax.random.normal(jax.random.fold_in(key, 5), array_shape, jnp.float32), -4.0, 4.0)
    return drawn_values.astype(jnp.bfloat16)


def draw_key_states(key, part):
    array_shape = (SEQUENCE_COUNT, SEQUENCE_LENGTH, KVH * HD)
    drawn_values = jnp.clip(jax.random.normal(jax.random.fold_in(key, 6), array_shape, jnp.float32), -4.0, 4.0)
    return drawn_values.astype(jnp.bfloat16)


def draw_step_bias(key, part):
    slow_share = 0.5
    slow_mask = jax.random.uniform(jax.random.fold_in(key, 11), (DI,), jnp.float32) < slow_share
    spread = jnp.exp(0.3 * jnp.clip(jax.random.normal(jax.random.fold_in(key, 12), (DI,), jnp.float32), -2.0, 2.0))
    target = jnp.where(slow_mask, 0.5 / SEQUENCE_LENGTH, 0.025) * spread
    return jnp.log(jnp.expm1(target)).astype(jnp.float32)


def draw_step_input(key, part):
    array_shape = (SEQUENCE_COUNT, SEQUENCE_LENGTH, DI)
    random_component = 0.5 * jnp.clip(jax.random.normal(jax.random.fold_in(key, 21), array_shape, jnp.float32), -4.0, 4.0)
    spike_row_list = jnp.arange(4, dtype=jnp.int32)[None, :] * (SEQUENCE_LENGTH // 4) + jax.random.randint(jax.random.fold_in(key, 22), (SEQUENCE_COUNT, 4), 0, SEQUENCE_LENGTH // 4)
    spike_flags = jnp.zeros((SEQUENCE_COUNT, SEQUENCE_LENGTH), jnp.float32).at[jnp.arange(SEQUENCE_COUNT)[:, None], spike_row_list].set(1.0)
    spike_increase = math.log(2.0 * SEQUENCE_LENGTH) - 0.87
    return (random_component + spike_increase * spike_flags[:, :, None]).astype(jnp.bfloat16)


def draw_state_proj(key, part):
    array_shape = (SEQUENCE_COUNT, SEQUENCE_LENGTH, DSTATE)
    level_sign = jnp.where(jax.random.bernoulli(jax.random.fold_in(key, 31), 0.5, (DSTATE,)), 1.0, -1.0)
    level = level_sign * jax.random.uniform(jax.random.fold_in(key, 32), (DSTATE,), jnp.float32, 0.5, 1.0)
    inflow = level[None, None, :] + 0.5 * jnp.clip(jax.random.normal(jax.random.fold_in(key, 33), array_shape, jnp.float32), -4.0, 4.0)
    readout = jnp.clip(jax.random.normal(jax.random.fold_in(key, 34), array_shape, jnp.float32), -4.0, 4.0)
    return jnp.concatenate([inflow, readout], axis=2).astype(jnp.bfloat16)


def draw_lengths(key, part):
    drawn_lengths = jax.random.randint(jax.random.fold_in(key, 41), (SEQUENCE_COUNT,), SEQUENCE_LENGTH // 4, SEQUENCE_LENGTH + 1)
    full_index = jax.random.randint(jax.random.fold_in(key, 42), (), 0, SEQUENCE_COUNT)
    return drawn_lengths.at[full_index].set(SEQUENCE_LENGTH).astype(jnp.int32)


def level_of(own_key, dims, shards, low, top_value):
    factor_of = 1.0
    for dim, parts in shards:
        draws = jax.random.uniform(jax.random.fold_in(jax.random.fold_in(own_key, 6), dim), (parts,), jnp.float32, low / len(shards), top_value / len(shards))
        factor_of = factor_of * jnp.repeat(jnp.exp(draws), dims[dim] // parts).reshape((-1,) + (1,) * (len(dims) - 1 - dim))
    return factor_of


def scatter_about(own_key, shape, scale, bound, shards=(), kind=jnp.bfloat16):
    drawn = scale * jax.random.normal(own_key, shape, jnp.float32)
    if shards:
        drawn = drawn * level_of(own_key, shape, shards, -0.22, 0.18)
    return jnp.clip(drawn, -bound, bound).astype(kind)


def setup_inputs(seed: int = 0) -> dict:
    keys = jax.random.split(jax.random.key(seed), 14)
    mixer_input = scatter_about(keys[0], (SEQUENCE_COUNT, SEQUENCE_LENGTH, DI), 1.0, 6.0, ((1, 256),))
    gate_input = scatter_about(keys[1], (SEQUENCE_COUNT, SEQUENCE_LENGTH, DI), 1.0, 6.0, ((1, 256),))
    step_input = draw_step_input(jax.random.fold_in(keys[13], 71), 0)
    state_proj = draw_state_proj(jax.random.fold_in(keys[13], 71), 0)
    conv_weight = scatter_about(keys[4], (CONV, DI), CONV ** -0.5, 3.0)
    conv_bias = jnp.clip(jax.random.uniform(keys[5], (DI,), jnp.float32, -1.0, 1.0), -1.0, 1.0)
    step_bias = draw_step_bias(jax.random.fold_in(keys[13], 71), 0)
    decay_log = jnp.clip(jax.random.uniform(keys[7], (DSTATE, DI), jnp.float32, -0.7, 0.7) * level_of(keys[7], (DSTATE, DI), ((1, 4),), -0.4, 0.0), -0.7, 0.7)
    skip_gain = jnp.clip(0.5 + 1.0 * jax.random.uniform(keys[8], (DI,), jnp.float32) ** level_of(keys[8], (DI,), ((0, 4),), -0.2, 0.2), 0.5, 1.5)
    query_states = draw_query_states(jax.random.fold_in(keys[13], 71), 0)
    key_states = draw_key_states(jax.random.fold_in(keys[13], 71), 0)
    value_states = scatter_about(keys[11], (SEQUENCE_COUNT, SEQUENCE_LENGTH, KVH * HD), 1.0, 6.0, ((1, 256),))
    lengths = draw_lengths(jax.random.fold_in(keys[13], 71), 0)
    return dict(mixer_input=mixer_input, gate_input=gate_input, step_input=step_input, state_proj=state_proj, conv_weight=conv_weight, conv_bias=conv_bias, step_bias=step_bias, decay_log=decay_log, skip_gain=skip_gain, query_states=query_states, key_states=key_states, value_states=value_states, lengths=lengths)


neg_large = -1e+30

def conv_rows(padded, conv_weight, conv_bias, row_count):
    running = jnp.zeros((padded.shape[0], row_count, padded.shape[2]), jnp.float32) + conv_bias[None, None, :]
    for tap_index in range(conv_weight.shape[0]):
        window = padded[:, tap_index:tap_index + row_count, :].astype(jnp.float32)
        running = running + window * conv_weight[tap_index].astype(jnp.float32)[None, None, :]
    return jax.nn.silu(running).astype(jnp.bfloat16)

def mixer(mixer_input, gate_input, step_input, state_proj, conv_weight, conv_bias, step_bias, decay_log, skip_gain):
    tap_count = conv_weight.shape[0]
    batch_size, row_count, channel_count = mixer_input.shape
    leading = jnp.zeros((batch_size, tap_count - 1, channel_count), mixer_input.dtype)
    padded = jnp.concatenate([leading, mixer_input], axis=1)
    conv_out = conv_rows(padded, conv_weight, conv_bias, row_count)
    decay_rate = jnp.exp(decay_log)
    projection = state_proj.astype(jnp.float32)
    inflow = projection[:, :, :DSTATE]
    readout = projection[:, :, DSTATE:]

    def advance(state_now, inputs):
        conv_row, step_row, inflow_row, readout_row, gate_row = inputs
        step_size = jax.nn.softplus(step_row.astype(jnp.float32) + step_bias[None, :])
        decay_now = jnp.exp(-step_size[:, None, :] * decay_rate[None])
        conv_value = conv_row.astype(jnp.float32)
        state_now = decay_now * state_now + (step_size * conv_value)[:, None, :] * inflow_row[:, :, None]
        mixed_rows = lax.optimization_barrier(jnp.sum(readout_row[:, :, None] * state_now, axis=1)) + skip_gain[None, :] * conv_value
        gated = mixed_rows * jax.nn.silu(gate_row.astype(jnp.float32))
        return (state_now, gated.astype(jnp.bfloat16))
    sequence_first = tuple((jnp.swapaxes(component, 0, 1) for component in (conv_out, step_input, inflow, readout, gate_input)))
    start_state = jnp.zeros((batch_size, DSTATE, channel_count), jnp.float32)
    _, outputs = lax.scan(advance, start_state, sequence_first)
    return jnp.swapaxes(outputs, 0, 1)

def attention(query_states, key_states, value_states):
    batch_size, row_count, _ = query_states.shape
    query_heads = jnp.transpose(query_states.reshape(batch_size, row_count, QH, HD), (2, 0, 1, 3))
    key_heads = jnp.transpose(key_states.reshape(batch_size, row_count, KVH, HD), (2, 0, 1, 3))
    value_heads = jnp.transpose(value_states.reshape(batch_size, row_count, KVH, HD), (2, 0, 1, 3))
    group_size = QH // KVH
    positions = jnp.arange(row_count, dtype=jnp.int32)
    allowed = positions[None, :] <= positions[:, None]
    logit_scale_factor = 1.0 / math.sqrt(HD)

    def one_head(head_index):
        single_query = query_heads[head_index].astype(jnp.float32)
        single_key = key_heads[head_index // group_size].astype(jnp.float32)
        single_value = value_heads[head_index // group_size].astype(jnp.float32)
        score_matrix = jnp.einsum('cog,cug->cou', single_query, single_key) * logit_scale_factor
        score_matrix = jnp.where(allowed[None], score_matrix, neg_large)
        row_peak = lax.optimization_barrier(jnp.max(score_matrix, axis=-1, keepdims=True))
        weights = jnp.where(allowed[None], jnp.exp(score_matrix - row_peak), 0.0)
        softmax_divisor = lax.optimization_barrier(jnp.sum(weights, axis=-1, keepdims=True))
        rounded_values = lax.optimization_barrier(weights.astype(jnp.bfloat16)).astype(jnp.float32)
        final_output = jnp.einsum('ziy,zyv->ziv', rounded_values, single_value) / softmax_divisor
        return final_output.astype(jnp.bfloat16)
    outputs = lax.map(one_head, jnp.arange(QH, dtype=jnp.int32))
    return jnp.transpose(outputs, (1, 2, 0, 3)).reshape(batch_size, row_count, QH * HD)

def reference(mixer_input, gate_input, step_input, state_proj, conv_weight, conv_bias, step_bias, decay_log, skip_gain, query_states, key_states, value_states, lengths):
    mixed_rows = mixer(mixer_input, gate_input, step_input, state_proj, conv_weight, conv_bias, step_bias, decay_log, skip_gain)
    attended = attention(query_states, key_states, value_states)
    live_rows = jnp.arange(SEQUENCE_LENGTH, dtype=jnp.int32)[None, :] < lengths[:, None]
    mixer_output = jnp.where(live_rows[:, :, None], mixed_rows, jnp.zeros((), jnp.bfloat16)).astype(jnp.bfloat16)
    attention_output = jnp.where(live_rows[:, :, None], attended, jnp.zeros((), jnp.bfloat16)).astype(jnp.bfloat16)
    return (mixer_output, attention_output)
```

```python
import functools
import math

import jax
import jax.numpy as jnp
from jax import lax
from jax.experimental import pallas as pl
from jax.experimental.pallas import tpu as pltpu
from jax.sharding import Mesh, PartitionSpec as P

HD = 128
LANES = 128
PIECES = 8
ROWS = 16
SPAN = PIECES * ROWS
WIDE = 1024
NST = 16
MSG = 24
LOG2E = math.log2(math.e)
neg_large = -1e30

F32 = jnp.float32
BF16 = jnp.bfloat16


def silu(v):
    return v / (1.0 + jnp.exp(-v))


def softplus(v):
    z = jnp.exp(-jnp.abs(v))
    u = 1.0 + z
    small = jnp.where(u == 1.0, z, jnp.log(u) * (z / jnp.where(u == 1.0, 1.0, u - 1.0)))
    return jnp.maximum(v, 0.0) + small


def row_of(ref, row):
    return jnp.broadcast_to(ref[0, pl.ds(row, 1), :], (8, LANES))


def first_pass(order, *refs):
    pieces = refs[:PIECES]
    tail, params, rate, inflow, dt_out, conv_out, msg_out, xf, sf, tmp = refs[PIECES:]
    for d in range(PIECES):
        at = pl.multiple_of(order[d] * ROWS, ROWS)
        xf[pl.ds(8 + at, ROWS), :] = pieces[d][0, 0].astype(F32)
        sf[pl.ds(at, ROWS), :] = pieces[d][1, 0].astype(F32)
    xf[5:8, :] = tail[0].astype(F32)
    for j in range(8):
        cols = slice(j * LANES, (j + 1) * LANES)
        acc = jnp.broadcast_to(params[4:5, cols], (SPAN, LANES))
        for k in range(4):
            acc = acc + xf[5 + k : 5 + k + SPAN, cols] * params[k : k + 1, cols]
        conv_out[0, 0, pl.ds(j, SPAN, stride=8), :] = silu(acc).astype(BF16).astype(F32)
        dt_out[0, 0, pl.ds(j, SPAN, stride=8), :] = softplus(sf[:, cols] + params[5:6, cols])
    rates = [rate[0, n] for n in range(NST)]

    def step(t, carry):
        states, elapsed = carry
        dt = dt_out[0, 0, pl.ds(pl.multiple_of(t * 8, 8), 8), :]
        u = dt * conv_out[0, 0, pl.ds(pl.multiple_of(t * 8, 8), 8), :]
        new = []
        for n in range(NST):
            new.append(jnp.exp2(dt * rates[n]) * states[n] + u * row_of(inflow, t * NST + n))
        return tuple(new), elapsed + dt

    zero = jnp.zeros((8, LANES), F32)
    states, elapsed = lax.fori_loop(0, SPAN, step, ((zero,) * NST, zero), unroll=2)
    for n in range(NST):
        tmp[pl.ds(n, 8, stride=MSG), :] = states[n]
    high = elapsed.astype(BF16).astype(F32)
    rest = elapsed - high
    middle = rest.astype(BF16).astype(F32)
    for n, part in enumerate((high, middle, rest - middle, zero, zero, zero, zero, zero)):
        tmp[pl.ds(NST + n, 8, stride=MSG), :] = part
    for j in range(8):
        msg_out[j] = tmp[j * MSG : (j + 1) * MSG, :].astype(BF16)


def prefix_pass(msg, rate, out):
    rates = rate[...]
    state = jnp.zeros((NST, LANES), F32)
    for s in range(msg.shape[0]):
        out[s] = state.astype(BF16)
        part = msg[s].astype(F32)
        elapsed = part[NST : NST + 1] + part[NST + 1 : NST + 2] + part[NST + 2 : NST + 3]
        state = jnp.exp2(rates * elapsed) * state + part[:NST]


def second_pass(order, *refs):
    gates = refs[:PIECES]
    dt_in, conv_in, params, rate, inflow, readout, entering, live, out, gf, ys, tmp = refs[PIECES:]
    for d in range(PIECES):
        at = pl.multiple_of(order[d] * ROWS, ROWS)
        gf[pl.ds(at, ROWS), :] = gates[d][0, 0].astype(F32)
    for j in range(8):
        tmp[j * NST : (j + 1) * NST, :] = entering[j].astype(F32)
    rates = [rate[0, n] for n in range(NST)]

    def step(t, states):
        dt = dt_in[0, 0, pl.ds(pl.multiple_of(t * 8, 8), 8), :]
        u = dt * conv_in[0, 0, pl.ds(pl.multiple_of(t * 8, 8), 8), :]
        new = []
        total = [None] * 4
        for n in range(NST):
            s = jnp.exp2(dt * rates[n]) * states[n] + u * row_of(inflow, t * NST + n)
            new.append(s)
            term = s * row_of(readout, t * NST + n)
            total[n % 4] = term if total[n % 4] is None else total[n % 4] + term
        ys[pl.ds(pl.multiple_of(t * 8, 8), 8), :] = (total[0] + total[1]) + (total[2] + total[3])
        return tuple(new)

    start = tuple(tmp[pl.ds(n, 8, stride=NST), :] for n in range(NST))
    lax.fori_loop(0, SPAN, step, start, unroll=2)
    rows = order[PIECES] + lax.broadcasted_iota(jnp.int32, (SPAN, LANES), 0)
    keep = rows < live[pl.program_id(1)]
    for j in range(8):
        cols = slice(j * LANES, (j + 1) * LANES)
        conv = conv_in[0, 0, pl.ds(j, SPAN, stride=8), :]
        mixed = ys[pl.ds(j, SPAN, stride=8), :] + params[6:7, cols] * conv
        gated = mixed * silu(gf[:, cols])
        out[0, :, cols] = jnp.where(keep, gated, 0.0).astype(BF16)


def pack_pass(q, k, v, out):
    for i in range(16):
        b, kvl, y = i // 8, (i // 4) % 2, i % 4
        g = 2 * y + kvl
        out[i, :, :1024] = q[b, :, g * 1024 : (g + 1) * 1024]
        out[i, :, 1024:1152] = k[b, :, g * HD : (g + 1) * HD]
        out[i, :, 1152:1280] = v[b, :, g * HD : (g + 1) * HD]


def attend_pass(info, q_ref, kv_ref, out):
    z, core, live = info[0], info[1], info[2]
    qs = q_ref[...].reshape(256, HD)
    factor = LOG2E / math.sqrt(HD)

    def block(zz, carry, masked):
        peak, divisor, acc = carry
        kv = kv_ref[pl.ds(zz * 2, 2)].reshape(512, 256)
        keys, values = kv[:, :HD], kv[:, HD:]
        scores = lax.dot_general(keys, qs, (((1,), (1,)), ((), ())), preferred_element_type=F32) * factor
        if masked:
            kr = lax.broadcasted_iota(jnp.int32, (512, 256), 0)
            qr = lax.broadcasted_iota(jnp.int32, (512, 256), 1)
            kp = ((kr // 64) % 4) * 128 + (kr // 256) * 64 + kr % 64
            qp = (qr // 64) * 128 + core * 64 + qr % 64
            scores = jnp.where(kp <= qp, scores, neg_large)
        new_peak = jnp.maximum(peak, jnp.max(scores, axis=0, keepdims=True))
        weights = jnp.exp2(scores - new_peak)
        fade = jnp.exp2(peak - new_peak)
        divisor = divisor * fade + jnp.sum(weights, axis=0, keepdims=True)
        update = lax.dot_general(
            values, weights.astype(BF16), (((0,), (0,)), ((), ())), preferred_element_type=F32
        )
        return new_peak, divisor, acc * fade + update

    start = (jnp.full((1, 256), neg_large, F32), jnp.zeros((1, 256), F32), jnp.zeros((HD, 256), F32))
    carry = lax.fori_loop(0, z, lambda zz, c: block(zz, c, False), start)
    _, divisor, acc = block(z, carry, True)
    result = jnp.transpose(acc / divisor)
    r = lax.broadcasted_iota(jnp.int32, (256, HD), 0)
    pos = z * 512 + (r // 64) * 128 + core * 64 + r % 64
    out[...] = jnp.where(pos < live, result, 0.0).astype(BF16).reshape(4, 64, HD)


def shards(
    mixer_input,
    gate_input,
    step_input,
    state_proj,
    conv_weight,
    conv_bias,
    step_bias,
    decay_log,
    skip_gain,
    query_states,
    key_states,
    value_states,
    lengths,
):
    z, x, core, head = (lax.axis_index(name) for name in ("z", "x", "core", "head"))
    nz, nx = lax.axis_size("z"), lax.axis_size("x")
    group = ("core", "head")
    half = decay_log.shape[1] // 2
    quarter = decay_log.shape[1]
    vmem = pl.BlockSpec(memory_space=pltpu.VMEM)

    packed = pl.pallas_call(
        pack_pass,
        out_shape=jax.ShapeDtypeStruct((16, ROWS, 1280), BF16),
        in_specs=[vmem] * 3,
        out_specs=vmem,
    )(query_states, key_states, value_states)

    def piece_for(to_core, to_head):
        at = to_head * quarter + to_core * half
        return jnp.stack(
            [
                lax.dynamic_slice_in_dim(part, at, half, 2)
                for part in (mixer_input, step_input, gate_input)
            ]
        )

    pieces, order = [], []
    for dc in range(2):
        for dh in range(4):
            block = piece_for(core ^ dc, (head + dh) % 4)
            route = [
                (c * 4 + h, (c ^ dc) * 4 + (h + dh) % 4) for c in range(2) for h in range(4)
            ]
            pieces.append(block if dc + dh == 0 else lax.ppermute(block, group, route))
            order.append((core ^ dc) * 4 + (head - dh) % 4)
    last = sum(
        jnp.where(order[d] == PIECES - 1, pieces[d][0, :, ROWS - 3 :, :], jnp.zeros((), BF16))
        for d in range(PIECES)
    )
    chips = nz * nx
    tail = lax.ppermute(last, ("z", "x"), [(i, i + 1) for i in range(chips - 1)])

    received = lax.all_to_all(packed, ("x", "head"), 0, 0, tiled=True)
    received = received.reshape(4, 64, 1280)
    kv_own = received[:, :, 1024:].reshape(1, 256, 256)
    kv_all = lax.all_gather(kv_own, ("z", "core"), axis=0, tiled=True)

    other = lax.ppermute(state_proj, "core", [(0, 1), (1, 0)])
    first = jnp.where(core == 0, state_proj, other)
    second = jnp.where(core == 0, other, state_proj)
    proj = jnp.concatenate([first, second], axis=1).astype(F32)
    inflow = jnp.broadcast_to(proj[:, :, :NST, None], (2, SPAN, NST, LANES)).reshape(2, SPAN * NST, LANES)
    readout = jnp.broadcast_to(proj[:, :, NST:, None], (2, SPAN, NST, LANES)).reshape(2, SPAN * NST, LANES)
    mine = lambda part, dim: lax.dynamic_slice_in_dim(part, core * half, half, dim)
    whole = lambda part, dim: lax.dynamic_slice_in_dim(part, head * quarter + core * half, half, dim)
    params = jnp.concatenate(
        [
            whole(conv_weight, 1).astype(F32),
            whole(conv_bias, 0)[None],
            mine(step_bias, 0)[None],
            mine(skip_gain, 0)[None],
            jnp.zeros((1, half), F32),
        ]
    )
    rate_rows = -LOG2E * jnp.exp(mine(decay_log, 1))
    rate = jnp.transpose(rate_rows.reshape(NST, 2, 8, LANES), (1, 0, 2, 3))
    start_row = (z * nx + x) * SPAN
    order = jnp.stack(order + [start_row]).astype(jnp.int32)

    blk = lambda arrays, which: pl.BlockSpec(
        (arrays, 1, ROWS, WIDE), lambda c, b, o: (which, b, 0, c)
    )
    slab = pl.BlockSpec((1, 1, SPAN * 8, LANES), lambda c, b, o: (b, c, 0, 0))
    params_spec = pl.BlockSpec((8, WIDE), lambda c, b, o: (0, c))
    rate_spec = pl.BlockSpec((1, NST, 8, LANES), lambda c, b, o: (c, 0, 0, 0))
    flow_spec = pl.BlockSpec((1, SPAN * NST, LANES), lambda c, b, o: (b, 0, 0))
    slab_shape = jax.ShapeDtypeStruct((2, 2, SPAN * 8, LANES), F32)
    dt, conv, message = pl.pallas_call(
        first_pass,
        grid_spec=pltpu.PrefetchScalarGridSpec(
            num_scalar_prefetch=1,
            grid=(2, 2),
            in_specs=[blk(2, 0)] * PIECES
            + [
                pl.BlockSpec((1, 3, WIDE), lambda c, b, o: (b, 0, c)),
                params_spec,
                rate_spec,
                flow_spec,
            ],
            out_specs=[
                slab,
                slab,
                pl.BlockSpec((8, MSG, LANES), lambda c, b, o: (b * 2 + c, 0, 0)),
            ],
            scratch_shapes=[
                pltpu.VMEM((SPAN + 8, WIDE), F32),
                pltpu.VMEM((SPAN, WIDE), F32),
                pltpu.VMEM((8 * MSG, LANES), F32),
            ],
        ),
        out_shape=[slab_shape, slab_shape, jax.ShapeDtypeStruct((32, MSG, LANES), BF16)],
        name="first_pass",
    )(order, *pieces, tail, params, rate, inflow)

    sections = lax.all_to_all(message, ("z", "x"), 0, 0, tiled=True)
    chunk = (z * nx + x) % 16
    rate_chunk = lax.dynamic_slice_in_dim(rate_rows, chunk * LANES, LANES, 1)
    prefix = pl.pallas_call(
        prefix_pass,
        out_shape=jax.ShapeDtypeStruct((32, NST, LANES), BF16),
        in_specs=[vmem] * 2,
        out_specs=vmem,
        name="prefix_pass",
    )(sections, rate_chunk)
    entering = lax.all_to_all(prefix, ("z", "x"), 0, 0, tiled=True)

    mixed = pl.pallas_call(
        second_pass,
        grid_spec=pltpu.PrefetchScalarGridSpec(
            num_scalar_prefetch=1,
            grid=(2, 2),
            in_specs=[blk(1, 2)] * PIECES
            + [
                slab,
                slab,
                params_spec,
                rate_spec,
                flow_spec,
                flow_spec,
                pl.BlockSpec((8, NST, LANES), lambda c, b, o: (b * 2 + c, 0, 0)),
                pl.BlockSpec(memory_space=pltpu.SMEM),
            ],
            out_specs=pl.BlockSpec((1, SPAN, WIDE), lambda c, b, o: (b, 0, c)),
            scratch_shapes=[
                pltpu.VMEM((SPAN, WIDE), F32),
                pltpu.VMEM((SPAN * 8, LANES), F32),
                pltpu.VMEM((8 * NST, LANES), F32),
            ],
        ),
        out_shape=jax.ShapeDtypeStruct((2, SPAN, half), BF16),
        name="second_pass",
    )(order, *pieces, dt, conv, params, rate, inflow, readout, entering, lengths)

    rows = SPAN // 2
    own = lax.dynamic_slice_in_dim(mixed, core * rows, rows, 1)
    away = lax.dynamic_slice_in_dim(mixed, (1 - core) * rows, rows, 1)
    back = lax.ppermute(away, "core", [(0, 1), (1, 0)])
    mixer_output = jnp.concatenate(
        [jnp.where(core == 0, own, back), jnp.where(core == 0, back, own)], axis=2
    )

    info = jnp.stack([z, core, lax.dynamic_index_in_dim(lengths, x // 2, 0, keepdims=False)])
    attended = pl.pallas_call(
        attend_pass,
        grid_spec=pltpu.PrefetchScalarGridSpec(
            num_scalar_prefetch=1,
            grid=(8,),
            in_specs=[
                pl.BlockSpec((4, 64, HD), lambda h, i: (0, 0, h)),
                pl.BlockSpec((16, 256, 256), lambda h, i: (0, 0, 0)),
            ],
            out_specs=pl.BlockSpec((4, 64, HD), lambda h, i: (0, 0, h)),
        ),
        out_shape=jax.ShapeDtypeStruct((4, 64, 1024), BF16),
        name="attend_pass",
    )(info.astype(jnp.int32), received, kv_all)
    home = lax.all_to_all(attended, "x", 0, 0, tiled=True)
    attention_output = jnp.stack(
        [
            jnp.concatenate([home[0], home[1]], axis=1),
            jnp.concatenate([home[2], home[3]], axis=1),
        ]
    )
    return (mixer_output, attention_output)


def solution(mesh):
    ctx = ("z", "x", "core")
    split = Mesh(mesh.devices.reshape(8, 4, 2, 4), ctx + ("head",))
    rows = P(None, ctx + ("head",), None)
    in_specs = (
        rows,
        rows,
        rows,
        P(None, ctx, None),
        P(),
        P(),
        P("head"),
        P(None, "head"),
        P("head"),
        rows,
        rows,
        rows,
        P(),
    )
    out_specs = (P(None, ctx, "head"), P(None, ctx, "head"))
    return jax.shard_map(shards, mesh=split, in_specs=in_specs, out_specs=out_specs, check_vma=False)
```

```python
import functools
import math

import jax
import jax.numpy as jnp
from jax import lax
from jax.experimental import pallas as pl
from jax.experimental.pallas import tpu as pltpu
from jax.sharding import Mesh, PartitionSpec as P

HD = 128
LANES = 128
PIECES = 8
ROWS = 16
SPAN = PIECES * ROWS
WIDE = 1024
NST = 16
MSG = 24
LOG2E = math.log2(math.e)
neg_large = -1e30

F32 = jnp.float32
BF16 = jnp.bfloat16


def silu(v):
    return v / (1.0 + jnp.exp(-v))


def softplus(v):
    z = jnp.exp(-jnp.abs(v))
    u = 1.0 + z
    small = jnp.where(u == 1.0, z, jnp.log(u) * (z / jnp.where(u == 1.0, 1.0, u - 1.0)))
    return jnp.maximum(v, 0.0) + small


def row_of(ref, row):
    return jnp.broadcast_to(ref[0, pl.ds(row, 1), :], (8, LANES))


def first_pass(order, *refs):
    pieces = refs[:PIECES]
    tail, params, rate, inflow, dt_out, conv_out, msg_out, xf, sf, tmp = refs[PIECES:]
    for d in range(PIECES):
        at = pl.multiple_of(order[d] * ROWS, ROWS)
        xf[pl.ds(8 + at, ROWS), :] = pieces[d][0, 0].astype(F32)
        sf[pl.ds(at, ROWS), :] = pieces[d][1, 0].astype(F32)
    xf[5:8, :] = tail[0].astype(F32)
    for j in range(8):
        cols = slice(j * LANES, (j + 1) * LANES)
        acc = jnp.broadcast_to(params[4:5, cols], (SPAN, LANES))
        for k in range(4):
            acc = acc + xf[5 + k : 5 + k + SPAN, cols] * params[k : k + 1, cols]
        conv_out[0, 0, pl.ds(j, SPAN, stride=8), :] = silu(acc).astype(BF16).astype(F32)
        dt_out[0, 0, pl.ds(j, SPAN, stride=8), :] = softplus(sf[:, cols] + params[5:6, cols])
    rates = [rate[0, n] for n in range(NST)]

    def step(t, carry):
        states, elapsed = carry
        dt = dt_out[0, 0, pl.ds(pl.multiple_of(t * 8, 8), 8), :]
        u = dt * conv_out[0, 0, pl.ds(pl.multiple_of(t * 8, 8), 8), :]
        new = []
        for n in range(NST):
            new.append(jnp.exp2(dt * rates[n]) * states[n] + u * row_of(inflow, t * NST + n))
        return tuple(new), elapsed + dt

    zero = jnp.zeros((8, LANES), F32)
    states, elapsed = lax.fori_loop(0, SPAN, step, ((zero,) * NST, zero), unroll=2)
    for n in range(NST):
        tmp[pl.ds(n, 8, stride=MSG), :] = states[n]
    high = elapsed.astype(BF16).astype(F32)
    rest = elapsed - high
    middle = rest.astype(BF16).astype(F32)
    for n, part in enumerate((high, middle, rest - middle, zero, zero, zero, zero, zero)):
        tmp[pl.ds(NST + n, 8, stride=MSG), :] = part
    for j in range(8):
        msg_out[j] = tmp[j * MSG : (j + 1) * MSG, :].astype(BF16)


def prefix_pass(msg, rate, out):
    rates = rate[...]
    state = jnp.zeros((NST, LANES), F32)
    for s in range(msg.shape[0]):
        out[s] = state.astype(BF16)
        part = msg[s].astype(F32)
        elapsed = part[NST : NST + 1] + part[NST + 1 : NST + 2] + part[NST + 2 : NST + 3]
        state = jnp.exp2(rates * elapsed) * state + part[:NST]


def second_pass(order, *refs):
    gates = refs[:PIECES]
    dt_in, conv_in, params, rate, inflow, readout, entering, live, out, gf, ys, tmp = refs[PIECES:]
    for d in range(PIECES):
        at = pl.multiple_of(order[d] * ROWS, ROWS)
        gf[pl.ds(at, ROWS), :] = gates[d][0, 0].astype(F32)
    for j in range(8):
        tmp[j * NST : (j + 1) * NST, :] = entering[j].astype(F32)
    rates = [rate[0, n] for n in range(NST)]

    def step(t, states):
        dt = dt_in[0, 0, pl.ds(pl.multiple_of(t * 8, 8), 8), :]
        u = dt * conv_in[0, 0, pl.ds(pl.multiple_of(t * 8, 8), 8), :]
        new = []
        total = [None] * 4
        for n in range(NST):
            s = jnp.exp2(dt * rates[n]) * states[n] + u * row_of(inflow, t * NST + n)
            new.append(s)
            term = s * row_of(readout, t * NST + n)
            total[n % 4] = term if total[n % 4] is None else total[n % 4] + term
        ys[pl.ds(pl.multiple_of(t * 8, 8), 8), :] = (total[0] + total[1]) + (total[2] + total[3])
        return tuple(new)

    start = tuple(tmp[pl.ds(n, 8, stride=NST), :] for n in range(NST))
    lax.fori_loop(0, SPAN, step, start, unroll=2)
    rows = order[PIECES] + lax.broadcasted_iota(jnp.int32, (SPAN, LANES), 0)
    keep = rows < live[pl.program_id(1)]
    for j in range(8):
        cols = slice(j * LANES, (j + 1) * LANES)
        conv = conv_in[0, 0, pl.ds(j, SPAN, stride=8), :]
        mixed = ys[pl.ds(j, SPAN, stride=8), :] + params[6:7, cols] * conv
        gated = mixed * silu(gf[:, cols])
        out[0, :, cols] = jnp.where(keep, gated, 0.0).astype(BF16)


def pack_pass(q, k, v, out):
    for i in range(16):
        b, kvl, y = i // 8, (i // 4) % 2, i % 4
        g = 2 * y + kvl
        out[i, :, :1024] = q[b, :, g * 1024 : (g + 1) * 1024]
        out[i, :, 1024:1152] = k[b, :, g * HD : (g + 1) * HD]
        out[i, :, 1152:1280] = v[b, :, g * HD : (g + 1) * HD]


def attend_pass(info, own_ref, far_ref, kv_ref, own_out, far_out):
    own = pl.program_id(0) < 2
    z, core, live = jnp.where(own, info[0], info[1]), info[2], info[3]
    qs = jnp.where(own, own_ref[...], far_ref[...]).reshape(256, HD)
    factor = LOG2E / math.sqrt(HD)

    def block(zz, carry, masked):
        peak, divisor, acc = carry
        kv = kv_ref[pl.ds(zz * 2, 2)].reshape(512, 256)
        keys, values = kv[:, :HD], kv[:, HD:]
        scores = lax.dot_general(keys, qs, (((1,), (1,)), ((), ())), preferred_element_type=F32) * factor
        if masked:
            kr = lax.broadcasted_iota(jnp.int32, (512, 256), 0)
            qr = lax.broadcasted_iota(jnp.int32, (512, 256), 1)
            kp = ((kr // 64) % 4) * 128 + (kr // 256) * 64 + kr % 64
            qp = (qr // 64) * 128 + core * 64 + qr % 64
            scores = jnp.where(kp <= qp, scores, neg_large)
        new_peak = jnp.maximum(peak, jnp.max(scores, axis=0, keepdims=True))
        weights = jnp.exp2(scores - new_peak)
        fade = jnp.exp2(peak - new_peak)
        divisor = divisor * fade + jnp.sum(weights, axis=0, keepdims=True)
        update = lax.dot_general(
            values, weights.astype(BF16), (((0,), (0,)), ((), ())), preferred_element_type=F32
        )
        return new_peak, divisor, acc * fade + update

    start = (jnp.full((1, 256), neg_large, F32), jnp.zeros((1, 256), F32), jnp.zeros((HD, 256), F32))
    carry = lax.fori_loop(0, z, lambda zz, c: block(zz, c, False), start)
    _, divisor, acc = block(z, carry, True)
    result = jnp.transpose(acc / divisor)
    r = lax.broadcasted_iota(jnp.int32, (256, HD), 0)
    pos = z * 512 + (r // 64) * 128 + core * 64 + r % 64
    kept = jnp.where(pos < live, result, 0.0).astype(BF16).reshape(4, 64, HD)

    @pl.when(own)
    def _():
        own_out[...] = kept

    @pl.when(jnp.logical_not(own))
    def _():
        far_out[...] = kept


def attend(part, info, own, far, kv):
    own_at = lambda i: jnp.minimum(i, 1)
    far_at = lambda i: jnp.maximum(i - 2, 0)
    block = lambda at, base: pl.BlockSpec((4, 64, HD), lambda i, o: (0, 0, base + at(i)))
    shape = jax.ShapeDtypeStruct((4, 64, 256), BF16)
    return pl.pallas_call(
        attend_pass,
        grid_spec=pltpu.PrefetchScalarGridSpec(
            num_scalar_prefetch=1,
            grid=(4,),
            in_specs=[
                block(own_at, 2 * part),
                block(far_at, 2 * part),
                pl.BlockSpec((16, 256, 256), lambda i, o: (0, 0, 0)),
            ],
            out_specs=[block(own_at, 0), block(far_at, 0)],
        ),
        out_shape=[shape, shape],
        name="attend_pass",
    )(info, own, far, kv)


def shards(
    mixer_input,
    gate_input,
    step_input,
    state_proj,
    conv_weight,
    conv_bias,
    step_bias,
    decay_log,
    skip_gain,
    query_states,
    key_states,
    value_states,
    lengths,
):
    z, x, core, head = (lax.axis_index(name) for name in ("z", "x", "core", "head"))
    nz, nx = lax.axis_size("z"), lax.axis_size("x")
    group = ("core", "head")
    half = decay_log.shape[1] // 2
    quarter = decay_log.shape[1]
    vmem = pl.BlockSpec(memory_space=pltpu.VMEM)

    packed = pl.pallas_call(
        pack_pass,
        out_shape=jax.ShapeDtypeStruct((16, ROWS, 1280), BF16),
        in_specs=[vmem] * 3,
        out_specs=vmem,
    )(query_states, key_states, value_states)

    def piece_for(to_core, to_head):
        at = to_head * quarter + to_core * half
        return jnp.stack(
            [
                lax.dynamic_slice_in_dim(part, at, half, 2)
                for part in (mixer_input, step_input, gate_input)
            ]
        )

    pieces, order = [], []
    for dc in range(2):
        for dh in range(4):
            block = piece_for(core ^ dc, (head + dh) % 4)
            route = [
                (c * 4 + h, (c ^ dc) * 4 + (h + dh) % 4) for c in range(2) for h in range(4)
            ]
            pieces.append(block if dc + dh == 0 else lax.ppermute(block, group, route))
            order.append((core ^ dc) * 4 + (head - dh) % 4)
    last = sum(
        jnp.where(order[d] == PIECES - 1, pieces[d][0, :, ROWS - 3 :, :], jnp.zeros((), BF16))
        for d in range(PIECES)
    )
    chips = nz * nx
    tail = lax.ppermute(last, ("z", "x"), [(i, i + 1) for i in range(chips - 1)])

    received = lax.all_to_all(packed, ("x", "head"), 0, 0, tiled=True)
    received = received.reshape(4, 64, 1280)
    kv_own = received[:, :, 1024:].reshape(1, 256, 256)
    kv_all = lax.all_gather(kv_own, ("z", "core"), axis=0, tiled=True)
    mirror = [(i, nz - 1 - i) for i in range(nz)]
    far = lax.ppermute(received[:, :, 512:1024], "z", mirror)
    info = jnp.stack(
        [z, nz - 1 - z, core, lax.dynamic_index_in_dim(lengths, x // 2, 0, keepdims=False)]
    ).astype(jnp.int32)

    other = lax.ppermute(state_proj, "core", [(0, 1), (1, 0)])
    first = jnp.where(core == 0, state_proj, other)
    second = jnp.where(core == 0, other, state_proj)
    proj = jnp.concatenate([first, second], axis=1).astype(F32)
    inflow = jnp.broadcast_to(proj[:, :, :NST, None], (2, SPAN, NST, LANES)).reshape(2, SPAN * NST, LANES)
    readout = jnp.broadcast_to(proj[:, :, NST:, None], (2, SPAN, NST, LANES)).reshape(2, SPAN * NST, LANES)
    mine = lambda part, dim: lax.dynamic_slice_in_dim(part, core * half, half, dim)
    whole = lambda part, dim: lax.dynamic_slice_in_dim(part, head * quarter + core * half, half, dim)
    params = jnp.concatenate(
        [
            whole(conv_weight, 1).astype(F32),
            whole(conv_bias, 0)[None],
            mine(step_bias, 0)[None],
            mine(skip_gain, 0)[None],
            jnp.zeros((1, half), F32),
        ]
    )
    rate_rows = -LOG2E * jnp.exp(mine(decay_log, 1))
    rate = jnp.transpose(rate_rows.reshape(NST, 2, 8, LANES), (1, 0, 2, 3))
    start_row = (z * nx + x) * SPAN
    order = jnp.stack(order + [start_row]).astype(jnp.int32)

    blk = lambda arrays, which: pl.BlockSpec(
        (arrays, 1, ROWS, WIDE), lambda c, b, o: (which, b, 0, c)
    )
    slab = pl.BlockSpec((1, 1, SPAN * 8, LANES), lambda c, b, o: (b, c, 0, 0))
    params_spec = pl.BlockSpec((8, WIDE), lambda c, b, o: (0, c))
    rate_spec = pl.BlockSpec((1, NST, 8, LANES), lambda c, b, o: (c, 0, 0, 0))
    flow_spec = pl.BlockSpec((1, SPAN * NST, LANES), lambda c, b, o: (b, 0, 0))
    slab_shape = jax.ShapeDtypeStruct((2, 2, SPAN * 8, LANES), F32)
    dt, conv, message = pl.pallas_call(
        first_pass,
        grid_spec=pltpu.PrefetchScalarGridSpec(
            num_scalar_prefetch=1,
            grid=(2, 2),
            in_specs=[blk(2, 0)] * PIECES
            + [
                pl.BlockSpec((1, 3, WIDE), lambda c, b, o: (b, 0, c)),
                params_spec,
                rate_spec,
                flow_spec,
            ],
            out_specs=[
                slab,
                slab,
                pl.BlockSpec((8, MSG, LANES), lambda c, b, o: (b * 2 + c, 0, 0)),
            ],
            scratch_shapes=[
                pltpu.VMEM((SPAN + 8, WIDE), F32),
                pltpu.VMEM((SPAN, WIDE), F32),
                pltpu.VMEM((8 * MSG, LANES), F32),
            ],
        ),
        out_shape=[slab_shape, slab_shape, jax.ShapeDtypeStruct((32, MSG, LANES), BF16)],
        name="first_pass",
    )(order, *pieces, tail, params, rate, inflow)

    message, far = lax.optimization_barrier((message, far))
    sections = lax.all_to_all(message, ("z", "x"), 0, 0, tiled=True)
    own_0, far_0 = attend(0, info, received, far, kv_all)
    sections, own_0, far_0 = lax.optimization_barrier((sections, own_0, far_0))
    back_0 = lax.ppermute(far_0, "z", mirror)
    chunk = (z * nx + x) % 16
    rate_chunk = lax.dynamic_slice_in_dim(rate_rows, chunk * LANES, LANES, 1)
    prefix = pl.pallas_call(
        prefix_pass,
        out_shape=jax.ShapeDtypeStruct((32, NST, LANES), BF16),
        in_specs=[vmem] * 2,
        out_specs=vmem,
        name="prefix_pass",
    )(sections, rate_chunk)
    prefix, far = lax.optimization_barrier((prefix, far))
    entering = lax.all_to_all(prefix, ("z", "x"), 0, 0, tiled=True)
    own_1, far_1 = attend(1, info, received, far, kv_all)
    entering, own_1, far_1, back_0 = lax.optimization_barrier((entering, own_1, far_1, back_0))
    back_1 = lax.ppermute(far_1, "z", mirror)

    mixed = pl.pallas_call(
        second_pass,
        grid_spec=pltpu.PrefetchScalarGridSpec(
            num_scalar_prefetch=1,
            grid=(2, 2),
            in_specs=[blk(1, 2)] * PIECES
            + [
                slab,
                slab,
                params_spec,
                rate_spec,
                flow_spec,
                flow_spec,
                pl.BlockSpec((8, NST, LANES), lambda c, b, o: (b * 2 + c, 0, 0)),
                pl.BlockSpec(memory_space=pltpu.SMEM),
            ],
            out_specs=pl.BlockSpec((1, SPAN, WIDE), lambda c, b, o: (b, 0, c)),
            scratch_shapes=[
                pltpu.VMEM((SPAN, WIDE), F32),
                pltpu.VMEM((SPAN * 8, LANES), F32),
                pltpu.VMEM((8 * NST, LANES), F32),
            ],
        ),
        out_shape=jax.ShapeDtypeStruct((2, SPAN, half), BF16),
        name="second_pass",
    )(order, *pieces, dt, conv, params, rate, inflow, readout, entering, lengths)

    rows = SPAN // 2
    own = lax.dynamic_slice_in_dim(mixed, core * rows, rows, 1)
    away = lax.dynamic_slice_in_dim(mixed, (1 - core) * rows, rows, 1)
    back = lax.ppermute(away, "core", [(0, 1), (1, 0)])
    mixer_output = jnp.concatenate(
        [jnp.where(core == 0, own, back), jnp.where(core == 0, back, own)], axis=2
    )

    attended = jnp.concatenate([own_0, own_1, back_0, back_1], axis=2)
    home = lax.all_to_all(attended, "x", 0, 0, tiled=True)
    attention_output = jnp.stack(
        [
            jnp.concatenate([home[0], home[1]], axis=1),
            jnp.concatenate([home[2], home[3]], axis=1),
        ]
    )
    return (mixer_output, attention_output)


def solution(mesh):
    ctx = ("z", "x", "core")
    split = Mesh(mesh.devices.reshape(8, 4, 2, 4), ctx + ("head",))
    rows = P(None, ctx + ("head",), None)
    in_specs = (
        rows,
        rows,
        rows,
        P(None, ctx, None),
        P(),
        P(),
        P("head"),
        P(None, "head"),
        P("head"),
        rows,
        rows,
        rows,
        P(),
    )
    out_specs = (P(None, ctx, "head"), P(None, ctx, "head"))
    return jax.shard_map(shards, mesh=split, in_specs=in_specs, out_specs=out_specs, check_vma=False)
```

```python
import functools
import math

import jax
import jax.numpy as jnp
from jax import lax
from jax.experimental import pallas as pl
from jax.experimental.pallas import tpu as pltpu
from jax.sharding import Mesh, PartitionSpec as P

HD = 128
LANES = 128
PIECES = 8
ROWS = 16
SPAN = PIECES * ROWS
WIDE = 1024
NST = 16
MSG = 24
LOG2E = math.log2(math.e)
neg_large = -1e30

F32 = jnp.float32
BF16 = jnp.bfloat16


def silu(v):
    return v / (1.0 + jnp.exp(-v))


def softplus(v):
    z = jnp.exp(-jnp.abs(v))
    u = 1.0 + z
    small = jnp.where(u == 1.0, z, jnp.log(u) * (z / jnp.where(u == 1.0, 1.0, u - 1.0)))
    return jnp.maximum(v, 0.0) + small


def row_of(ref, row):
    return jnp.broadcast_to(ref[0, pl.ds(row, 1), :], (8, LANES))


def first_pass(order, *refs):
    pieces = refs[:PIECES]
    tail, params, rate, inflow, dt_out, conv_out, msg_out, xf, sf, tmp = refs[PIECES:]
    for d in range(PIECES):
        at = pl.multiple_of(order[d] * ROWS, ROWS)
        xf[pl.ds(8 + at, ROWS), :] = pieces[d][0, 0].astype(F32)
        sf[pl.ds(at, ROWS), :] = pieces[d][1, 0].astype(F32)
    xf[5:8, :] = tail[0].astype(F32)
    for j in range(8):
        cols = slice(j * LANES, (j + 1) * LANES)
        acc = jnp.broadcast_to(params[4:5, cols], (SPAN, LANES))
        for k in range(4):
            acc = acc + xf[5 + k : 5 + k + SPAN, cols] * params[k : k + 1, cols]
        conv_out[0, 0, pl.ds(j, SPAN, stride=8), :] = silu(acc).astype(BF16).astype(F32)
        dt_out[0, 0, pl.ds(j, SPAN, stride=8), :] = softplus(sf[:, cols] + params[5:6, cols])
    rates = [rate[0, n] for n in range(NST)]

    def step(t, carry):
        states, elapsed = carry
        dt = dt_out[0, 0, pl.ds(pl.multiple_of(t * 8, 8), 8), :]
        u = dt * conv_out[0, 0, pl.ds(pl.multiple_of(t * 8, 8), 8), :]
        new = []
        for n in range(NST):
            new.append(jnp.exp2(dt * rates[n]) * states[n] + u * row_of(inflow, t * NST + n))
        return tuple(new), elapsed + dt

    zero = jnp.zeros((8, LANES), F32)
    states, elapsed = lax.fori_loop(0, SPAN, step, ((zero,) * NST, zero), unroll=2)
    for n in range(NST):
        tmp[pl.ds(n, 8, stride=MSG), :] = states[n]
    high = elapsed.astype(BF16).astype(F32)
    rest = elapsed - high
    middle = rest.astype(BF16).astype(F32)
    for n, part in enumerate((high, middle, rest - middle, zero, zero, zero, zero, zero)):
        tmp[pl.ds(NST + n, 8, stride=MSG), :] = part
    for j in range(8):
        msg_out[j] = tmp[j * MSG : (j + 1) * MSG, :].astype(BF16)


def prefix_pass(msg, rate, out):
    rates = rate[...]
    state = jnp.zeros((NST, LANES), F32)
    for s in range(msg.shape[0]):
        out[s] = state.astype(BF16)
        part = msg[s].astype(F32)
        elapsed = part[NST : NST + 1] + part[NST + 1 : NST + 2] + part[NST + 2 : NST + 3]
        state = jnp.exp2(rates * elapsed) * state + part[:NST]


def second_pass(order, *refs):
    gates = refs[:PIECES]
    dt_in, conv_in, params, rate, inflow, readout, entering, live, out, gf, ys, tmp = refs[PIECES:]
    for d in range(PIECES):
        at = pl.multiple_of(order[d] * ROWS, ROWS)
        gf[pl.ds(at, ROWS), :] = gates[d][0, 0].astype(F32)
    for j in range(8):
        tmp[j * NST : (j + 1) * NST, :] = entering[j].astype(F32)
    rates = [rate[0, n] for n in range(NST)]

    def step(t, states):
        dt = dt_in[0, 0, pl.ds(pl.multiple_of(t * 8, 8), 8), :]
        u = dt * conv_in[0, 0, pl.ds(pl.multiple_of(t * 8, 8), 8), :]
        new = []
        total = [None] * 4
        for n in range(NST):
            s = jnp.exp2(dt * rates[n]) * states[n] + u * row_of(inflow, t * NST + n)
            new.append(s)
            term = s * row_of(readout, t * NST + n)
            total[n % 4] = term if total[n % 4] is None else total[n % 4] + term
        ys[pl.ds(pl.multiple_of(t * 8, 8), 8), :] = (total[0] + total[1]) + (total[2] + total[3])
        return tuple(new)

    start = tuple(tmp[pl.ds(n, 8, stride=NST), :] for n in range(NST))
    lax.fori_loop(0, SPAN, step, start, unroll=2)
    rows = order[PIECES] + lax.broadcasted_iota(jnp.int32, (SPAN, LANES), 0)
    keep = rows < live[pl.program_id(1)]
    for j in range(8):
        cols = slice(j * LANES, (j + 1) * LANES)
        conv = conv_in[0, 0, pl.ds(j, SPAN, stride=8), :]
        mixed = ys[pl.ds(j, SPAN, stride=8), :] + params[6:7, cols] * conv
        gated = mixed * silu(gf[:, cols])
        out[0, :, cols] = jnp.where(keep, gated, 0.0).astype(BF16)


def pack_pass(q, k, v, out):
    for i in range(16):
        b, kvl, y = i // 8, (i // 4) % 2, i % 4
        g = 2 * y + kvl
        out[i, :, :1024] = q[b, :, g * 1024 : (g + 1) * 1024]
        out[i, :, 1024:1152] = k[b, :, g * HD : (g + 1) * HD]
        out[i, :, 1152:1280] = v[b, :, g * HD : (g + 1) * HD]


def attend_pass(info, own_ref, far_ref, kv_ref, own_out, far_out):
    own = pl.program_id(0) < 2
    z, core, live = jnp.where(own, info[0], info[1]), info[2], info[3]
    qs = jnp.where(own, own_ref[...], far_ref[...]).reshape(256, HD)
    factor = LOG2E / math.sqrt(HD)

    def block(zz, carry, masked):
        peak, divisor, acc = carry
        kv = kv_ref[pl.ds(zz * 2, 2)].reshape(512, 256)
        keys, values = kv[:, :HD], kv[:, HD:]
        scores = lax.dot_general(keys, qs, (((1,), (1,)), ((), ())), preferred_element_type=F32) * factor
        if masked:
            kr = lax.broadcasted_iota(jnp.int32, (512, 256), 0)
            qr = lax.broadcasted_iota(jnp.int32, (512, 256), 1)
            kp = ((kr // 64) % 4) * 128 + (kr // 256) * 64 + kr % 64
            qp = (qr // 64) * 128 + core * 64 + qr % 64
            scores = jnp.where(kp <= qp, scores, neg_large)
        new_peak = jnp.maximum(peak, jnp.max(scores, axis=0, keepdims=True))
        weights = jnp.exp2(scores - new_peak)
        fade = jnp.exp2(peak - new_peak)
        divisor = divisor * fade + jnp.sum(weights, axis=0, keepdims=True)
        update = lax.dot_general(
            values, weights.astype(BF16), (((0,), (0,)), ((), ())), preferred_element_type=F32
        )
        return new_peak, divisor, acc * fade + update

    start = (jnp.full((1, 256), neg_large, F32), jnp.zeros((1, 256), F32), jnp.zeros((HD, 256), F32))
    carry = lax.fori_loop(0, z, lambda zz, c: block(zz, c, False), start)
    _, divisor, acc = block(z, carry, True)
    result = jnp.transpose(acc / divisor)
    r = lax.broadcasted_iota(jnp.int32, (256, HD), 0)
    pos = z * 512 + (r // 64) * 128 + core * 64 + r % 64
    kept = jnp.where(pos < live, result, 0.0).astype(BF16).reshape(4, 64, HD)

    @pl.when(own)
    def _():
        own_out[...] = kept

    @pl.when(jnp.logical_not(own))
    def _():
        far_out[...] = kept


def attend(part, info, own, far, kv):
    own_at = lambda i: jnp.minimum(i, 1)
    far_at = lambda i: jnp.maximum(i - 2, 0)
    block = lambda at, base: pl.BlockSpec((4, 64, HD), lambda i, o: (0, 0, base + at(i)))
    shape = jax.ShapeDtypeStruct((4, 64, 256), BF16)
    return pl.pallas_call(
        attend_pass,
        grid_spec=pltpu.PrefetchScalarGridSpec(
            num_scalar_prefetch=1,
            grid=(4,),
            in_specs=[
                block(own_at, 2 * part),
                block(far_at, 2 * part),
                pl.BlockSpec((16, 256, 256), lambda i, o: (0, 0, 0)),
            ],
            out_specs=[block(own_at, 0), block(far_at, 0)],
        ),
        out_shape=[shape, shape],
        name="attend_pass",
    )(info, own, far, kv)


def shards(
    mixer_input,
    gate_input,
    step_input,
    state_proj,
    conv_weight,
    conv_bias,
    step_bias,
    decay_log,
    skip_gain,
    query_states,
    key_states,
    value_states,
    lengths,
):
    z, x, core, head = (lax.axis_index(name) for name in ("z", "x", "core", "head"))
    nz, nx = lax.axis_size("z"), lax.axis_size("x")
    group = ("core", "head")
    half = decay_log.shape[1] // 2
    quarter = decay_log.shape[1]
    vmem = pl.BlockSpec(memory_space=pltpu.VMEM)

    turns = [(dc, dh) for dc in range(2) for dh in range(4)]

    def slice_for(part, turn):
        dc, dh = turn
        at = (head + dh) % 4 * quarter + (core ^ dc) * half
        return lax.dynamic_slice_in_dim(part, at, half, 2)

    def turned(block, turn):
        dc, dh = turn
        route = [(c * 4 + h, (c ^ dc) * 4 + (h + dh) % 4) for c in range(2) for h in range(4)]
        return block if dc + dh == 0 else lax.ppermute(block, group, route)

    pieces = [
        turned(jnp.stack([slice_for(mixer_input, turn), slice_for(step_input, turn)]), turn)
        for turn in turns
    ]
    order = [(core ^ dc) * 4 + (head - dh) % 4 for dc, dh in turns]
    packed = pl.pallas_call(
        pack_pass,
        out_shape=jax.ShapeDtypeStruct((16, ROWS, 1280), BF16),
        in_specs=[vmem] * 3,
        out_specs=vmem,
    )(query_states, key_states, value_states)
    received = lax.all_to_all(packed, ("x", "head"), 0, 0, tiled=True)
    received, pieces[:5] = lax.optimization_barrier((received, pieces[:5]))
    last = sum(
        jnp.where(order[d] == PIECES - 1, pieces[d][0, :, ROWS - 3 :, :], jnp.zeros((), BF16))
        for d in range(PIECES)
    )
    chips = nz * nx
    tail = lax.ppermute(last, ("z", "x"), [(i, i + 1) for i in range(chips - 1)])
    received = received.reshape(4, 64, 1280)
    kv_own = received[:, :, 1024:].reshape(1, 256, 256)
    kv_all = lax.all_gather(kv_own, ("z", "core"), axis=0, tiled=True)
    info = jnp.stack(
        [z, nz - 1 - z, core, lax.dynamic_index_in_dim(lengths, x // 2, 0, keepdims=False)]
    ).astype(jnp.int32)

    mirror = [(i, nz - 1 - i) for i in range(nz)]
    far, tail, gate_input = lax.optimization_barrier((received[:, :, 512:1024], tail, gate_input))
    far = lax.ppermute(far, "z", mirror)
    gates = [turned(slice_for(gate_input, turn)[None], turn) for turn in turns[:4]]

    other = lax.ppermute(state_proj, "core", [(0, 1), (1, 0)])
    first = jnp.where(core == 0, state_proj, other)
    second = jnp.where(core == 0, other, state_proj)
    proj = jnp.concatenate([first, second], axis=1).astype(F32)
    inflow = jnp.broadcast_to(proj[:, :, :NST, None], (2, SPAN, NST, LANES)).reshape(2, SPAN * NST, LANES)
    readout = jnp.broadcast_to(proj[:, :, NST:, None], (2, SPAN, NST, LANES)).reshape(2, SPAN * NST, LANES)
    mine = lambda part, dim: lax.dynamic_slice_in_dim(part, core * half, half, dim)
    whole = lambda part, dim: lax.dynamic_slice_in_dim(part, head * quarter + core * half, half, dim)
    params = jnp.concatenate(
        [
            whole(conv_weight, 1).astype(F32),
            whole(conv_bias, 0)[None],
            mine(step_bias, 0)[None],
            mine(skip_gain, 0)[None],
            jnp.zeros((1, half), F32),
        ]
    )
    rate_rows = -LOG2E * jnp.exp(mine(decay_log, 1))
    rate = jnp.transpose(rate_rows.reshape(NST, 2, 8, LANES), (1, 0, 2, 3))
    start_row = (z * nx + x) * SPAN
    order = jnp.stack(order + [start_row]).astype(jnp.int32)

    blk = lambda arrays: pl.BlockSpec((arrays, 1, ROWS, WIDE), lambda c, b, o: (0, b, 0, c))
    slab = pl.BlockSpec((1, 1, SPAN * 8, LANES), lambda c, b, o: (b, c, 0, 0))
    params_spec = pl.BlockSpec((8, WIDE), lambda c, b, o: (0, c))
    rate_spec = pl.BlockSpec((1, NST, 8, LANES), lambda c, b, o: (c, 0, 0, 0))
    flow_spec = pl.BlockSpec((1, SPAN * NST, LANES), lambda c, b, o: (b, 0, 0))
    slab_shape = jax.ShapeDtypeStruct((2, 2, SPAN * 8, LANES), F32)
    dt, conv, message = pl.pallas_call(
        first_pass,
        grid_spec=pltpu.PrefetchScalarGridSpec(
            num_scalar_prefetch=1,
            grid=(2, 2),
            in_specs=[blk(2)] * PIECES
            + [
                pl.BlockSpec((1, 3, WIDE), lambda c, b, o: (b, 0, c)),
                params_spec,
                rate_spec,
                flow_spec,
            ],
            out_specs=[
                slab,
                slab,
                pl.BlockSpec((8, MSG, LANES), lambda c, b, o: (b * 2 + c, 0, 0)),
            ],
            scratch_shapes=[
                pltpu.VMEM((SPAN + 8, WIDE), F32),
                pltpu.VMEM((SPAN, WIDE), F32),
                pltpu.VMEM((8 * MSG, LANES), F32),
            ],
        ),
        out_shape=[slab_shape, slab_shape, jax.ShapeDtypeStruct((32, MSG, LANES), BF16)],
        name="first_pass",
    )(order, *pieces, tail, params, rate, inflow)

    message, far, gates, gate_input = lax.optimization_barrier((message, far, gates, gate_input))
    late = [turned(slice_for(gate_input, turn)[None], turn) for turn in turns[4:]]
    sections = lax.all_to_all(message, ("z", "x"), 0, 0, tiled=True)
    own_0, far_0 = attend(0, info, received, far, kv_all)
    sections, own_0, far_0, late = lax.optimization_barrier((sections, own_0, far_0, late))
    gates = gates + late
    back_0 = lax.ppermute(far_0, "z", mirror)
    chunk = (z * nx + x) % 16
    rate_chunk = lax.dynamic_slice_in_dim(rate_rows, chunk * LANES, LANES, 1)
    prefix = pl.pallas_call(
        prefix_pass,
        out_shape=jax.ShapeDtypeStruct((32, NST, LANES), BF16),
        in_specs=[vmem] * 2,
        out_specs=vmem,
        name="prefix_pass",
    )(sections, rate_chunk)
    prefix, far = lax.optimization_barrier((prefix, far))
    entering = lax.all_to_all(prefix, ("z", "x"), 0, 0, tiled=True)
    own_1, far_1 = attend(1, info, received, far, kv_all)
    entering, own_1, far_1, back_0 = lax.optimization_barrier((entering, own_1, far_1, back_0))
    back_1 = lax.ppermute(far_1, "z", mirror)

    mixed = pl.pallas_call(
        second_pass,
        grid_spec=pltpu.PrefetchScalarGridSpec(
            num_scalar_prefetch=1,
            grid=(2, 2),
            in_specs=[blk(1)] * PIECES
            + [
                slab,
                slab,
                params_spec,
                rate_spec,
                flow_spec,
                flow_spec,
                pl.BlockSpec((8, NST, LANES), lambda c, b, o: (b * 2 + c, 0, 0)),
                pl.BlockSpec(memory_space=pltpu.SMEM),
            ],
            out_specs=pl.BlockSpec((1, SPAN, WIDE), lambda c, b, o: (b, 0, c)),
            scratch_shapes=[
                pltpu.VMEM((SPAN, WIDE), F32),
                pltpu.VMEM((SPAN * 8, LANES), F32),
                pltpu.VMEM((8 * NST, LANES), F32),
            ],
        ),
        out_shape=jax.ShapeDtypeStruct((2, SPAN, half), BF16),
        name="second_pass",
    )(order, *gates, dt, conv, params, rate, inflow, readout, entering, lengths)

    mixed, back_1 = lax.optimization_barrier((mixed, back_1))
    rows = SPAN // 2
    own = lax.dynamic_slice_in_dim(mixed, core * rows, rows, 1)
    away = lax.dynamic_slice_in_dim(mixed, (1 - core) * rows, rows, 1)
    back = lax.ppermute(away, "core", [(0, 1), (1, 0)])
    mixer_output = jnp.concatenate(
        [jnp.where(core == 0, own, back), jnp.where(core == 0, back, own)], axis=2
    )

    attended = jnp.concatenate([own_0, own_1, back_0, back_1], axis=2)
    home = lax.all_to_all(attended, "x", 0, 0, tiled=True)
    attention_output = jnp.stack(
        [
            jnp.concatenate([home[0], home[1]], axis=1),
            jnp.concatenate([home[2], home[3]], axis=1),
        ]
    )
    return (mixer_output, attention_output)


def solution(mesh):
    ctx = ("z", "x", "core")
    split = Mesh(mesh.devices.reshape(8, 4, 2, 4), ctx + ("head",))
    rows = P(None, ctx + ("head",), None)
    in_specs = (
        rows,
        rows,
        rows,
        P(None, ctx, None),
        P(),
        P(),
        P("head"),
        P(None, "head"),
        P("head"),
        rows,
        rows,
        rows,
        P(),
    )
    out_specs = (P(None, ctx, "head"), P(None, ctx, "head"))
    return jax.shard_map(shards, mesh=split, in_specs=in_specs, out_specs=out_specs, check_vma=False)
```

```python
import functools
import math

import jax
import jax.numpy as jnp
from jax import lax
from jax.experimental import pallas as pl
from jax.experimental.pallas import tpu as pltpu
from jax.sharding import Mesh, PartitionSpec as P

HD = 128
LANES = 128
PIECES = 8
ROWS = 16
SPAN = PIECES * ROWS
WIDE = 1024
NST = 16
MSG = 24
LOG2E = math.log2(math.e)
neg_large = -1e30

F32 = jnp.float32
BF16 = jnp.bfloat16


def silu(v):
    return v / (1.0 + jnp.exp(-v))


def softplus(v):
    z = jnp.exp(-jnp.abs(v))
    u = 1.0 + z
    small = jnp.where(u == 1.0, z, jnp.log(u) * (z / jnp.where(u == 1.0, 1.0, u - 1.0)))
    return jnp.maximum(v, 0.0) + small


def row_of(ref, row):
    return jnp.broadcast_to(ref[0, pl.ds(row, 1), :], (8, LANES))


def first_pass(order, *refs):
    pieces = refs[:PIECES]
    tail, params, rate, inflow, dt_out, conv_out, msg_out, xf, sf, tmp = refs[PIECES:]
    for d in range(PIECES):
        at = pl.multiple_of(order[d] * ROWS, ROWS)
        xf[pl.ds(8 + at, ROWS), :] = pieces[d][0, 0].astype(F32)
        sf[pl.ds(at, ROWS), :] = pieces[d][1, 0].astype(F32)
    xf[5:8, :] = tail[0].astype(F32)
    for j in range(8):
        cols = slice(j * LANES, (j + 1) * LANES)
        acc = jnp.broadcast_to(params[4:5, cols], (SPAN, LANES))
        for k in range(4):
            acc = acc + xf[5 + k : 5 + k + SPAN, cols] * params[k : k + 1, cols]
        conv_out[0, 0, pl.ds(j, SPAN, stride=8), :] = silu(acc).astype(BF16).astype(F32)
        dt_out[0, 0, pl.ds(j, SPAN, stride=8), :] = softplus(sf[:, cols] + params[5:6, cols])
    rates = [rate[0, n] for n in range(NST)]

    def step(t, carry):
        states, elapsed = carry
        dt = dt_out[0, 0, pl.ds(pl.multiple_of(t * 8, 8), 8), :]
        u = dt * conv_out[0, 0, pl.ds(pl.multiple_of(t * 8, 8), 8), :]
        new = []
        for n in range(NST):
            new.append(jnp.exp2(dt * rates[n]) * states[n] + u * row_of(inflow, t * NST + n))
        return tuple(new), elapsed + dt

    zero = jnp.zeros((8, LANES), F32)
    states, elapsed = lax.fori_loop(0, SPAN, step, ((zero,) * NST, zero), unroll=2)
    for n in range(NST):
        tmp[pl.ds(n, 8, stride=MSG), :] = states[n]
    high = elapsed.astype(BF16).astype(F32)
    rest = elapsed - high
    middle = rest.astype(BF16).astype(F32)
    for n, part in enumerate((high, middle, rest - middle, zero, zero, zero, zero, zero)):
        tmp[pl.ds(NST + n, 8, stride=MSG), :] = part
    for j in range(8):
        msg_out[j] = tmp[j * MSG : (j + 1) * MSG, :].astype(BF16)


def prefix_pass(msg, rate, out):
    rates = rate[...]
    state = jnp.zeros((NST, LANES), F32)
    for s in range(msg.shape[0]):
        out[s] = state.astype(BF16)
        part = msg[s].astype(F32)
        elapsed = part[NST : NST + 1] + part[NST + 1 : NST + 2] + part[NST + 2 : NST + 3]
        state = jnp.exp2(rates * elapsed) * state + part[:NST]


def second_pass(order, *refs):
    gates = refs[:PIECES]
    dt_in, conv_in, params, rate, inflow, readout, entering, live, out, gf, ys, tmp = refs[PIECES:]
    for d in range(PIECES):
        at = pl.multiple_of(order[d] * ROWS, ROWS)
        gf[pl.ds(at, ROWS), :] = gates[d][0, 0].astype(F32)
    for j in range(8):
        tmp[j * NST : (j + 1) * NST, :] = entering[j].astype(F32)
    rates = [rate[0, n] for n in range(NST)]

    def step(t, states):
        dt = dt_in[0, 0, pl.ds(pl.multiple_of(t * 8, 8), 8), :]
        u = dt * conv_in[0, 0, pl.ds(pl.multiple_of(t * 8, 8), 8), :]
        new = []
        total = [None] * 4
        for n in range(NST):
            s = jnp.exp2(dt * rates[n]) * states[n] + u * row_of(inflow, t * NST + n)
            new.append(s)
            term = s * row_of(readout, t * NST + n)
            total[n % 4] = term if total[n % 4] is None else total[n % 4] + term
        ys[pl.ds(pl.multiple_of(t * 8, 8), 8), :] = (total[0] + total[1]) + (total[2] + total[3])
        return tuple(new)

    start = tuple(tmp[pl.ds(n, 8, stride=NST), :] for n in range(NST))
    lax.fori_loop(0, SPAN, step, start, unroll=2)
    rows = order[PIECES] + lax.broadcasted_iota(jnp.int32, (SPAN, LANES), 0)
    keep = rows < live[pl.program_id(1)]
    for j in range(8):
        cols = slice(j * LANES, (j + 1) * LANES)
        conv = conv_in[0, 0, pl.ds(j, SPAN, stride=8), :]
        mixed = ys[pl.ds(j, SPAN, stride=8), :] + params[6:7, cols] * conv
        gated = mixed * silu(gf[:, cols])
        out[0, :, cols] = jnp.where(keep, gated, 0.0).astype(BF16)


def pack_pass(q, k, v, out):
    for i in range(16):
        b, kvl, y = i // 8, (i // 4) % 2, i % 4
        g = 2 * y + kvl
        out[i, :, :1024] = q[b, :, g * 1024 : (g + 1) * 1024]
        out[i, :, 1024:1152] = k[b, :, g * HD : (g + 1) * HD]
        out[i, :, 1152:1280] = v[b, :, g * HD : (g + 1) * HD]


def attend_pass(info, own_ref, far_ref, kv_ref, own_out, far_out):
    own = pl.program_id(0) == 0
    z, core, live = jnp.where(own, info[0], info[1]), info[2], info[3]
    both = jnp.where(own, own_ref[...], far_ref[...])
    qs = jnp.concatenate([both[:, :, :HD].reshape(256, HD), both[:, :, HD:].reshape(256, HD)])
    factor = LOG2E / math.sqrt(HD)

    def block(zz, carry, masked):
        peak, divisor, acc = carry
        kv = kv_ref[pl.ds(zz * 2, 2)].reshape(512, 256)
        keys, values = kv[:, :HD], kv[:, HD:]
        scores = lax.dot_general(keys, qs, (((1,), (1,)), ((), ())), preferred_element_type=F32) * factor
        if masked:
            kr = lax.broadcasted_iota(jnp.int32, (512, 512), 0)
            qr = lax.broadcasted_iota(jnp.int32, (512, 512), 1) % 256
            kp = ((kr // 64) % 4) * 128 + (kr // 256) * 64 + kr % 64
            qp = (qr // 64) * 128 + core * 64 + qr % 64
            scores = jnp.where(kp <= qp, scores, neg_large)
        new_peak = jnp.maximum(peak, jnp.max(scores, axis=0, keepdims=True))
        weights = jnp.exp2(scores - new_peak)
        fade = jnp.exp2(peak - new_peak)
        divisor = divisor * fade + jnp.sum(weights, axis=0, keepdims=True)
        update = lax.dot_general(
            values, weights.astype(BF16), (((0,), (0,)), ((), ())), preferred_element_type=F32
        )
        return new_peak, divisor, acc * fade + update

    start = (jnp.full((1, 512), neg_large, F32), jnp.zeros((1, 512), F32), jnp.zeros((HD, 512), F32))
    carry = lax.fori_loop(0, z, lambda zz, c: block(zz, c, False), start)
    _, divisor, acc = block(z, carry, True)
    result = jnp.transpose(acc / divisor)
    r = lax.broadcasted_iota(jnp.int32, (512, HD), 0) % 256
    pos = z * 512 + (r // 64) * 128 + core * 64 + r % 64
    kept = jnp.where(pos < live, result, 0.0).astype(BF16)
    kept = [kept[i * 256 : (i + 1) * 256].reshape(4, 64, HD) for i in range(2)]

    @pl.when(own)
    def _():
        own_out[:, :, :HD] = kept[0]
        own_out[:, :, HD:] = kept[1]

    @pl.when(jnp.logical_not(own))
    def _():
        far_out[:, :, :HD] = kept[0]
        far_out[:, :, HD:] = kept[1]


def attend(part, info, own, far, kv):
    block = lambda at: pl.BlockSpec((4, 64, 2 * HD), lambda i, o: (0, 0, at))
    shape = jax.ShapeDtypeStruct((4, 64, 256), BF16)
    return pl.pallas_call(
        attend_pass,
        grid_spec=pltpu.PrefetchScalarGridSpec(
            num_scalar_prefetch=1,
            grid=(2,),
            in_specs=[
                block(part),
                block(part),
                pl.BlockSpec((16, 256, 256), lambda i, o: (0, 0, 0)),
            ],
            out_specs=[block(0), block(0)],
        ),
        out_shape=[shape, shape],
        name="attend_pass",
    )(info, own, far, kv)


def shards(
    mixer_input,
    gate_input,
    step_input,
    state_proj,
    conv_weight,
    conv_bias,
    step_bias,
    decay_log,
    skip_gain,
    query_states,
    key_states,
    value_states,
    lengths,
):
    z, x, core, head = (lax.axis_index(name) for name in ("z", "x", "core", "head"))
    nz, nx = lax.axis_size("z"), lax.axis_size("x")
    group = ("core", "head")
    half = decay_log.shape[1] // 2
    quarter = decay_log.shape[1]
    vmem = pl.BlockSpec(memory_space=pltpu.VMEM)

    turns = [(dc, dh) for dc in range(2) for dh in range(4)]

    def slice_for(part, turn):
        dc, dh = turn
        at = (head + dh) % 4 * quarter + (core ^ dc) * half
        return lax.dynamic_slice_in_dim(part, at, half, 2)

    def turned(block, turn):
        dc, dh = turn
        route = [(c * 4 + h, (c ^ dc) * 4 + (h + dh) % 4) for c in range(2) for h in range(4)]
        return block if dc + dh == 0 else lax.ppermute(block, group, route)

    pieces = [
        turned(jnp.stack([slice_for(mixer_input, turn), slice_for(step_input, turn)]), turn)
        for turn in turns
    ]
    order = [(core ^ dc) * 4 + (head - dh) % 4 for dc, dh in turns]
    packed = pl.pallas_call(
        pack_pass,
        out_shape=jax.ShapeDtypeStruct((16, ROWS, 1280), BF16),
        in_specs=[vmem] * 3,
        out_specs=vmem,
    )(query_states, key_states, value_states)
    received = lax.all_to_all(packed, ("x", "head"), 0, 0, tiled=True)
    received, pieces[:5] = lax.optimization_barrier((received, pieces[:5]))
    last = sum(
        jnp.where(order[d] == PIECES - 1, pieces[d][0, :, ROWS - 3 :, :], jnp.zeros((), BF16))
        for d in range(PIECES)
    )
    chips = nz * nx
    last, gate_input = lax.optimization_barrier((last, gate_input))
    tail = lax.ppermute(last, ("z", "x"), [(i, i + 1) for i in range(chips - 1)])
    received = received.reshape(4, 64, 1280)
    kv_own = received[:, :, 1024:].reshape(1, 256, 256)
    kv_all = lax.all_gather(kv_own, ("z", "core"), axis=0, tiled=True)
    info = jnp.stack(
        [z, nz - 1 - z, core, lax.dynamic_index_in_dim(lengths, x // 2, 0, keepdims=False)]
    ).astype(jnp.int32)

    mirror = [(i, nz - 1 - i) for i in range(nz)]
    gates = [turned(slice_for(gate_input, turn)[None], turn) for turn in turns[:4]]

    other = lax.ppermute(state_proj, "core", [(0, 1), (1, 0)])
    first = jnp.where(core == 0, state_proj, other)
    second = jnp.where(core == 0, other, state_proj)
    proj = jnp.concatenate([first, second], axis=1).astype(F32)
    inflow = jnp.broadcast_to(proj[:, :, :NST, None], (2, SPAN, NST, LANES)).reshape(2, SPAN * NST, LANES)
    readout = jnp.broadcast_to(proj[:, :, NST:, None], (2, SPAN, NST, LANES)).reshape(2, SPAN * NST, LANES)
    far, tail, inflow = lax.optimization_barrier((received[:, :, 512:1024], tail, inflow))
    far = lax.ppermute(far, "z", mirror)
    mine = lambda part, dim: lax.dynamic_slice_in_dim(part, core * half, half, dim)
    whole = lambda part, dim: lax.dynamic_slice_in_dim(part, head * quarter + core * half, half, dim)
    params = jnp.concatenate(
        [
            whole(conv_weight, 1).astype(F32),
            whole(conv_bias, 0)[None],
            mine(step_bias, 0)[None],
            mine(skip_gain, 0)[None],
            jnp.zeros((1, half), F32),
        ]
    )
    rate_rows = -LOG2E * jnp.exp(mine(decay_log, 1))
    rate = jnp.transpose(rate_rows.reshape(NST, 2, 8, LANES), (1, 0, 2, 3))
    start_row = (z * nx + x) * SPAN
    order = jnp.stack(order + [start_row]).astype(jnp.int32)

    blk = lambda arrays: pl.BlockSpec((arrays, 1, ROWS, WIDE), lambda c, b, o: (0, b, 0, c))
    slab = pl.BlockSpec((1, 1, SPAN * 8, LANES), lambda c, b, o: (b, c, 0, 0))
    params_spec = pl.BlockSpec((8, WIDE), lambda c, b, o: (0, c))
    rate_spec = pl.BlockSpec((1, NST, 8, LANES), lambda c, b, o: (c, 0, 0, 0))
    flow_spec = pl.BlockSpec((1, SPAN * NST, LANES), lambda c, b, o: (b, 0, 0))
    slab_shape = jax.ShapeDtypeStruct((2, 2, SPAN * 8, LANES), F32)
    dt, conv, message = pl.pallas_call(
        first_pass,
        grid_spec=pltpu.PrefetchScalarGridSpec(
            num_scalar_prefetch=1,
            grid=(2, 2),
            in_specs=[blk(2)] * PIECES
            + [
                pl.BlockSpec((1, 3, WIDE), lambda c, b, o: (b, 0, c)),
                params_spec,
                rate_spec,
                flow_spec,
            ],
            out_specs=[
                slab,
                slab,
                pl.BlockSpec((8, MSG, LANES), lambda c, b, o: (b * 2 + c, 0, 0)),
            ],
            scratch_shapes=[
                pltpu.VMEM((SPAN + 8, WIDE), F32),
                pltpu.VMEM((SPAN, WIDE), F32),
                pltpu.VMEM((8 * MSG, LANES), F32),
            ],
        ),
        out_shape=[slab_shape, slab_shape, jax.ShapeDtypeStruct((32, MSG, LANES), BF16)],
        name="first_pass",
    )(order, *pieces, tail, params, rate, inflow)

    message, far, gates, gate_input = lax.optimization_barrier((message, far, gates, gate_input))
    late = [turned(slice_for(gate_input, turn)[None], turn) for turn in turns[4:]]
    sections = lax.all_to_all(message, ("z", "x"), 0, 0, tiled=True)
    own_0, far_0 = attend(0, info, received, far, kv_all)
    sections, own_0, far_0, late = lax.optimization_barrier((sections, own_0, far_0, late))
    gates = gates + late
    back_0 = lax.ppermute(far_0, "z", mirror)
    chunk = (z * nx + x) % 16
    rate_chunk = lax.dynamic_slice_in_dim(rate_rows, chunk * LANES, LANES, 1)
    prefix = pl.pallas_call(
        prefix_pass,
        out_shape=jax.ShapeDtypeStruct((32, NST, LANES), BF16),
        in_specs=[vmem] * 2,
        out_specs=vmem,
        name="prefix_pass",
    )(sections, rate_chunk)
    prefix, far = lax.optimization_barrier((prefix, far))
    entering = lax.all_to_all(prefix, ("z", "x"), 0, 0, tiled=True)
    own_1, far_1 = attend(1, info, received, far, kv_all)
    entering, own_1, far_1, back_0 = lax.optimization_barrier((entering, own_1, far_1, back_0))
    back_1 = lax.ppermute(far_1, "z", mirror)

    mixed = pl.pallas_call(
        second_pass,
        grid_spec=pltpu.PrefetchScalarGridSpec(
            num_scalar_prefetch=1,
            grid=(2, 2),
            in_specs=[blk(1)] * PIECES
            + [
                slab,
                slab,
                params_spec,
                rate_spec,
                flow_spec,
                flow_spec,
                pl.BlockSpec((8, NST, LANES), lambda c, b, o: (b * 2 + c, 0, 0)),
                pl.BlockSpec(memory_space=pltpu.SMEM),
            ],
            out_specs=pl.BlockSpec((1, SPAN, WIDE), lambda c, b, o: (b, 0, c)),
            scratch_shapes=[
                pltpu.VMEM((SPAN, WIDE), F32),
                pltpu.VMEM((SPAN * 8, LANES), F32),
                pltpu.VMEM((8 * NST, LANES), F32),
            ],
        ),
        out_shape=jax.ShapeDtypeStruct((2, SPAN, half), BF16),
        name="second_pass",
    )(order, *gates, dt, conv, params, rate, inflow, readout, entering, lengths)

    mixed, back_1 = lax.optimization_barrier((mixed, back_1))
    rows = SPAN // 2
    own = lax.dynamic_slice_in_dim(mixed, core * rows, rows, 1)
    away = lax.dynamic_slice_in_dim(mixed, (1 - core) * rows, rows, 1)
    back = lax.ppermute(away, "core", [(0, 1), (1, 0)])
    mixer_output = jnp.concatenate(
        [jnp.where(core == 0, own, back), jnp.where(core == 0, back, own)], axis=2
    )

    attended = jnp.concatenate([own_0, own_1, back_0, back_1], axis=2)
    home = lax.all_to_all(attended, "x", 0, 0, tiled=True)
    attention_output = jnp.stack(
        [
            jnp.concatenate([home[0], home[1]], axis=1),
            jnp.concatenate([home[2], home[3]], axis=1),
        ]
    )
    return (mixer_output, attention_output)


def solution(mesh):
    ctx = ("z", "x", "core")
    split = Mesh(mesh.devices.reshape(8, 4, 2, 4), ctx + ("head",))
    rows = P(None, ctx + ("head",), None)
    in_specs = (
        rows,
        rows,
        rows,
        P(None, ctx, None),
        P(),
        P(),
        P("head"),
        P(None, "head"),
        P("head"),
        rows,
        rows,
        rows,
        P(),
    )
    out_specs = (P(None, ctx, "head"), P(None, ctx, "head"))
    return jax.shard_map(shards, mesh=split, in_specs=in_specs, out_specs=out_specs, check_vma=False)
```

```python
import functools
import math

import jax
import jax.numpy as jnp
from jax import lax
from jax.experimental import pallas as pl
from jax.experimental.pallas import tpu as pltpu
from jax.sharding import Mesh, PartitionSpec as P

HD = 128
LANES = 128
PIECES = 8
ROWS = 16
SPAN = PIECES * ROWS
WIDE = 1024
NST = 16
MSG = 24
LOG2E = math.log2(math.e)
neg_large = -1e30

F32 = jnp.float32
BF16 = jnp.bfloat16


def silu(v):
    return v / (1.0 + jnp.exp(-v))


def softplus(v):
    z = jnp.exp(-jnp.abs(v))
    u = 1.0 + z
    small = jnp.where(u == 1.0, z, jnp.log(u) * (z / jnp.where(u == 1.0, 1.0, u - 1.0)))
    return jnp.maximum(v, 0.0) + small


def row_of(ref, row):
    return jnp.broadcast_to(ref[0, pl.ds(row, 1), :], (8, LANES))


def first_pass(order, *refs):
    pieces = refs[:PIECES]
    tail, params, rate, inflow, dt_out, conv_out, msg_out, xf, sf, tmp = refs[PIECES:]
    for d in range(PIECES):
        at = pl.multiple_of(order[d] * ROWS, ROWS)
        xf[pl.ds(8 + at, ROWS), :] = pieces[d][0, 0].astype(F32)
        sf[pl.ds(at, ROWS), :] = pieces[d][1, 0].astype(F32)
    xf[5:8, :] = tail[0].astype(F32)
    for j in range(8):
        cols = slice(j * LANES, (j + 1) * LANES)
        acc = jnp.broadcast_to(params[4:5, cols], (SPAN, LANES))
        for k in range(4):
            acc = acc + xf[5 + k : 5 + k + SPAN, cols] * params[k : k + 1, cols]
        conv_out[0, 0, pl.ds(j, SPAN, stride=8), :] = silu(acc).astype(BF16).astype(F32)
        dt_out[0, 0, pl.ds(j, SPAN, stride=8), :] = softplus(sf[:, cols] + params[5:6, cols])
    rates = [rate[0, n] for n in range(NST)]

    def step(t, carry):
        states, elapsed = carry
        dt = dt_out[0, 0, pl.ds(pl.multiple_of(t * 8, 8), 8), :]
        u = dt * conv_out[0, 0, pl.ds(pl.multiple_of(t * 8, 8), 8), :]
        new = []
        for n in range(NST):
            new.append(jnp.exp2(dt * rates[n]) * states[n] + u * row_of(inflow, t * NST + n))
        return tuple(new), elapsed + dt

    zero = jnp.zeros((8, LANES), F32)
    states, elapsed = lax.fori_loop(0, SPAN, step, ((zero,) * NST, zero), unroll=4)
    for n in range(NST):
        tmp[pl.ds(n, 8, stride=MSG), :] = states[n]
    high = elapsed.astype(BF16).astype(F32)
    rest = elapsed - high
    middle = rest.astype(BF16).astype(F32)
    for n, part in enumerate((high, middle, rest - middle, zero, zero, zero, zero, zero)):
        tmp[pl.ds(NST + n, 8, stride=MSG), :] = part
    for j in range(8):
        msg_out[j] = tmp[j * MSG : (j + 1) * MSG, :].astype(BF16)


def prefix_pass(msg, rate, out):
    rates = rate[...]
    state = jnp.zeros((NST, LANES), F32)
    for s in range(msg.shape[0]):
        out[s] = state.astype(BF16)
        part = msg[s].astype(F32)
        elapsed = part[NST : NST + 1] + part[NST + 1 : NST + 2] + part[NST + 2 : NST + 3]
        state = jnp.exp2(rates * elapsed) * state + part[:NST]


def second_pass(order, *refs):
    gates = refs[:PIECES]
    dt_in, conv_in, params, rate, inflow, readout, entering, live, out, gf, ys, tmp = refs[PIECES:]
    for d in range(PIECES):
        at = pl.multiple_of(order[d] * ROWS, ROWS)
        gf[pl.ds(at, ROWS), :] = gates[d][0, 0].astype(F32)
    for j in range(8):
        tmp[j * NST : (j + 1) * NST, :] = entering[j].astype(F32)
    rates = [rate[0, n] for n in range(NST)]

    def step(t, states):
        dt = dt_in[0, 0, pl.ds(pl.multiple_of(t * 8, 8), 8), :]
        u = dt * conv_in[0, 0, pl.ds(pl.multiple_of(t * 8, 8), 8), :]
        new = []
        total = [None] * 4
        for n in range(NST):
            s = jnp.exp2(dt * rates[n]) * states[n] + u * row_of(inflow, t * NST + n)
            new.append(s)
            term = s * row_of(readout, t * NST + n)
            total[n % 4] = term if total[n % 4] is None else total[n % 4] + term
        ys[pl.ds(pl.multiple_of(t * 8, 8), 8), :] = (total[0] + total[1]) + (total[2] + total[3])
        return tuple(new)

    start = tuple(tmp[pl.ds(n, 8, stride=NST), :] for n in range(NST))
    lax.fori_loop(0, SPAN, step, start, unroll=4)
    rows = order[PIECES] + lax.broadcasted_iota(jnp.int32, (SPAN, LANES), 0)
    keep = rows < live[pl.program_id(1)]
    for j in range(8):
        cols = slice(j * LANES, (j + 1) * LANES)
        conv = conv_in[0, 0, pl.ds(j, SPAN, stride=8), :]
        mixed = ys[pl.ds(j, SPAN, stride=8), :] + params[6:7, cols] * conv
        gated = mixed * silu(gf[:, cols])
        out[0, :, cols] = jnp.where(keep, gated, 0.0).astype(BF16)


def pack_pass(q, k, v, out):
    for i in range(16):
        b, kvl, y = i // 8, (i // 4) % 2, i % 4
        g = 2 * y + kvl
        out[i, :, :1024] = q[b, :, g * 1024 : (g + 1) * 1024]
        out[i, :, 1024:1152] = k[b, :, g * HD : (g + 1) * HD]
        out[i, :, 1152:1280] = v[b, :, g * HD : (g + 1) * HD]


def attend_pass(info, own_ref, far_ref, kv_ref, own_out, far_out):
    own = pl.program_id(0) == 0
    z, core, live = jnp.where(own, info[0], info[1]), info[2], info[3]
    both = jnp.where(own, own_ref[...], far_ref[...])
    qs = jnp.concatenate([both[:, :, :HD].reshape(256, HD), both[:, :, HD:].reshape(256, HD)])
    factor = LOG2E / math.sqrt(HD)

    def block(zz, carry, masked):
        peak, divisor, acc = carry
        kv = kv_ref[pl.ds(zz * 2, 2)].reshape(512, 256)
        keys, values = kv[:, :HD], kv[:, HD:]
        scores = lax.dot_general(keys, qs, (((1,), (1,)), ((), ())), preferred_element_type=F32) * factor
        if masked:
            kr = lax.broadcasted_iota(jnp.int32, (512, 512), 0)
            qr = lax.broadcasted_iota(jnp.int32, (512, 512), 1) % 256
            kp = ((kr // 64) % 4) * 128 + (kr // 256) * 64 + kr % 64
            qp = (qr // 64) * 128 + core * 64 + qr % 64
            scores = jnp.where(kp <= qp, scores, neg_large)
        new_peak = jnp.maximum(peak, jnp.max(scores, axis=0, keepdims=True))
        weights = jnp.exp2(scores - new_peak)
        fade = jnp.exp2(peak - new_peak)
        divisor = divisor * fade + jnp.sum(weights, axis=0, keepdims=True)
        update = lax.dot_general(
            values, weights.astype(BF16), (((0,), (0,)), ((), ())), preferred_element_type=F32
        )
        return new_peak, divisor, acc * fade + update

    start = (jnp.full((1, 512), neg_large, F32), jnp.zeros((1, 512), F32), jnp.zeros((HD, 512), F32))
    carry = lax.fori_loop(0, z, lambda zz, c: block(zz, c, False), start)
    _, divisor, acc = block(z, carry, True)
    result = jnp.transpose(acc / divisor)
    r = lax.broadcasted_iota(jnp.int32, (512, HD), 0) % 256
    pos = z * 512 + (r // 64) * 128 + core * 64 + r % 64
    kept = jnp.where(pos < live, result, 0.0).astype(BF16)
    kept = [kept[i * 256 : (i + 1) * 256].reshape(4, 64, HD) for i in range(2)]

    @pl.when(own)
    def _():
        own_out[:, :, :HD] = kept[0]
        own_out[:, :, HD:] = kept[1]

    @pl.when(jnp.logical_not(own))
    def _():
        far_out[:, :, :HD] = kept[0]
        far_out[:, :, HD:] = kept[1]


def attend(part, info, own, far, kv):
    block = lambda at: pl.BlockSpec((4, 64, 2 * HD), lambda i, o: (0, 0, at))
    shape = jax.ShapeDtypeStruct((4, 64, 256), BF16)
    return pl.pallas_call(
        attend_pass,
        grid_spec=pltpu.PrefetchScalarGridSpec(
            num_scalar_prefetch=1,
            grid=(2,),
            in_specs=[
                block(part),
                block(part),
                pl.BlockSpec((16, 256, 256), lambda i, o: (0, 0, 0)),
            ],
            out_specs=[block(0), block(0)],
        ),
        out_shape=[shape, shape],
        name="attend_pass",
    )(info, own, far, kv)


def shards(
    mixer_input,
    gate_input,
    step_input,
    state_proj,
    conv_weight,
    conv_bias,
    step_bias,
    decay_log,
    skip_gain,
    query_states,
    key_states,
    value_states,
    lengths,
):
    z, x, core, head = (lax.axis_index(name) for name in ("z", "x", "core", "head"))
    nz, nx = lax.axis_size("z"), lax.axis_size("x")
    group = ("core", "head")
    half = decay_log.shape[1] // 2
    quarter = decay_log.shape[1]
    vmem = pl.BlockSpec(memory_space=pltpu.VMEM)

    turns = [(dc, dh) for dc in range(2) for dh in range(4)]

    def slice_for(part, turn):
        dc, dh = turn
        at = (head + dh) % 4 * quarter + (core ^ dc) * half
        return lax.dynamic_slice_in_dim(part, at, half, 2)

    def turned(block, turn):
        dc, dh = turn
        route = [(c * 4 + h, (c ^ dc) * 4 + (h + dh) % 4) for c in range(2) for h in range(4)]
        return block if dc + dh == 0 else lax.ppermute(block, group, route)

    pieces = [
        turned(jnp.stack([slice_for(mixer_input, turn), slice_for(step_input, turn)]), turn)
        for turn in turns
    ]
    order = [(core ^ dc) * 4 + (head - dh) % 4 for dc, dh in turns]
    packed = pl.pallas_call(
        pack_pass,
        out_shape=jax.ShapeDtypeStruct((16, ROWS, 1280), BF16),
        in_specs=[vmem] * 3,
        out_specs=vmem,
    )(query_states, key_states, value_states)
    received = lax.all_to_all(packed, ("x", "head"), 0, 0, tiled=True)
    received, pieces[:5] = lax.optimization_barrier((received, pieces[:5]))
    last = sum(
        jnp.where(order[d] == PIECES - 1, pieces[d][0, :, ROWS - 3 :, :], jnp.zeros((), BF16))
        for d in range(PIECES)
    )
    chips = nz * nx
    last, gate_input = lax.optimization_barrier((last, gate_input))
    tail = lax.ppermute(last, ("z", "x"), [(i, i + 1) for i in range(chips - 1)])
    received = received.reshape(4, 64, 1280)
    kv_own = received[:, :, 1024:].reshape(1, 256, 256)
    kv_all = lax.all_gather(kv_own, ("z", "core"), axis=0, tiled=True)
    info = jnp.stack(
        [z, nz - 1 - z, core, lax.dynamic_index_in_dim(lengths, x // 2, 0, keepdims=False)]
    ).astype(jnp.int32)

    mirror = [(i, nz - 1 - i) for i in range(nz)]
    gates = [turned(slice_for(gate_input, turn)[None], turn) for turn in turns[:4]]

    other = lax.ppermute(state_proj, "core", [(0, 1), (1, 0)])
    first = jnp.where(core == 0, state_proj, other)
    second = jnp.where(core == 0, other, state_proj)
    proj = jnp.concatenate([first, second], axis=1).astype(F32)
    inflow = jnp.broadcast_to(proj[:, :, :NST, None], (2, SPAN, NST, LANES)).reshape(2, SPAN * NST, LANES)
    readout = jnp.broadcast_to(proj[:, :, NST:, None], (2, SPAN, NST, LANES)).reshape(2, SPAN * NST, LANES)
    far, tail, inflow = lax.optimization_barrier((received[:, :, 512:1024], tail, inflow))
    far = lax.ppermute(far, "z", mirror)
    mine = lambda part, dim: lax.dynamic_slice_in_dim(part, core * half, half, dim)
    whole = lambda part, dim: lax.dynamic_slice_in_dim(part, head * quarter + core * half, half, dim)
    params = jnp.concatenate(
        [
            whole(conv_weight, 1).astype(F32),
            whole(conv_bias, 0)[None],
            mine(step_bias, 0)[None],
            mine(skip_gain, 0)[None],
            jnp.zeros((1, half), F32),
        ]
    )
    rate_rows = -LOG2E * jnp.exp(mine(decay_log, 1))
    rate = jnp.transpose(rate_rows.reshape(NST, 2, 8, LANES), (1, 0, 2, 3))
    start_row = (z * nx + x) * SPAN
    order = jnp.stack(order + [start_row]).astype(jnp.int32)

    blk = lambda arrays: pl.BlockSpec((arrays, 1, ROWS, WIDE), lambda c, b, o: (0, b, 0, c))
    slab = pl.BlockSpec((1, 1, SPAN * 8, LANES), lambda c, b, o: (b, c, 0, 0))
    params_spec = pl.BlockSpec((8, WIDE), lambda c, b, o: (0, c))
    rate_spec = pl.BlockSpec((1, NST, 8, LANES), lambda c, b, o: (c, 0, 0, 0))
    flow_spec = pl.BlockSpec((1, SPAN * NST, LANES), lambda c, b, o: (b, 0, 0))
    slab_shape = jax.ShapeDtypeStruct((2, 2, SPAN * 8, LANES), F32)
    dt, conv, message = pl.pallas_call(
        first_pass,
        grid_spec=pltpu.PrefetchScalarGridSpec(
            num_scalar_prefetch=1,
            grid=(2, 2),
            in_specs=[blk(2)] * PIECES
            + [
                pl.BlockSpec((1, 3, WIDE), lambda c, b, o: (b, 0, c)),
                params_spec,
                rate_spec,
                flow_spec,
            ],
            out_specs=[
                slab,
                slab,
                pl.BlockSpec((8, MSG, LANES), lambda c, b, o: (b * 2 + c, 0, 0)),
            ],
            scratch_shapes=[
                pltpu.VMEM((SPAN + 8, WIDE), F32),
                pltpu.VMEM((SPAN, WIDE), F32),
                pltpu.VMEM((8 * MSG, LANES), F32),
            ],
        ),
        out_shape=[slab_shape, slab_shape, jax.ShapeDtypeStruct((32, MSG, LANES), BF16)],
        name="first_pass",
    )(order, *pieces, tail, params, rate, inflow)

    message, far, gates, gate_input = lax.optimization_barrier((message, far, gates, gate_input))
    late = [turned(slice_for(gate_input, turn)[None], turn) for turn in turns[4:]]
    sections = lax.all_to_all(message, ("z", "x"), 0, 0, tiled=True)
    own_0, far_0 = attend(0, info, received, far, kv_all)
    sections, own_0, far_0, late = lax.optimization_barrier((sections, own_0, far_0, late))
    gates = gates + late
    back_0 = lax.ppermute(far_0, "z", mirror)
    chunk = (z * nx + x) % 16
    rate_chunk = lax.dynamic_slice_in_dim(rate_rows, chunk * LANES, LANES, 1)
    prefix = pl.pallas_call(
        prefix_pass,
        out_shape=jax.ShapeDtypeStruct((32, NST, LANES), BF16),
        in_specs=[vmem] * 2,
        out_specs=vmem,
        name="prefix_pass",
    )(sections, rate_chunk)
    prefix, far = lax.optimization_barrier((prefix, far))
    entering = lax.all_to_all(prefix, ("z", "x"), 0, 0, tiled=True)
    own_1, far_1 = attend(1, info, received, far, kv_all)
    entering, own_1, far_1, back_0 = lax.optimization_barrier((entering, own_1, far_1, back_0))
    back_1 = lax.ppermute(far_1, "z", mirror)

    mixed = pl.pallas_call(
        second_pass,
        grid_spec=pltpu.PrefetchScalarGridSpec(
            num_scalar_prefetch=1,
            grid=(2, 2),
            in_specs=[blk(1)] * PIECES
            + [
                slab,
                slab,
                params_spec,
                rate_spec,
                flow_spec,
                flow_spec,
                pl.BlockSpec((8, NST, LANES), lambda c, b, o: (b * 2 + c, 0, 0)),
                pl.BlockSpec(memory_space=pltpu.SMEM),
            ],
            out_specs=pl.BlockSpec((1, SPAN, WIDE), lambda c, b, o: (b, 0, c)),
            scratch_shapes=[
                pltpu.VMEM((SPAN, WIDE), F32),
                pltpu.VMEM((SPAN * 8, LANES), F32),
                pltpu.VMEM((8 * NST, LANES), F32),
            ],
        ),
        out_shape=jax.ShapeDtypeStruct((2, SPAN, half), BF16),
        name="second_pass",
    )(order, *gates, dt, conv, params, rate, inflow, readout, entering, lengths)

    mixed, back_1 = lax.optimization_barrier((mixed, back_1))
    rows = SPAN // 2
    own = lax.dynamic_slice_in_dim(mixed, core * rows, rows, 1)
    away = lax.dynamic_slice_in_dim(mixed, (1 - core) * rows, rows, 1)
    back = lax.ppermute(away, "core", [(0, 1), (1, 0)])
    mixer_output = jnp.concatenate(
        [jnp.where(core == 0, own, back), jnp.where(core == 0, back, own)], axis=2
    )

    attended = jnp.concatenate([own_0, own_1, back_0, back_1], axis=2)
    home = lax.all_to_all(attended, "x", 0, 0, tiled=True)
    attention_output = jnp.stack(
        [
            jnp.concatenate([home[0], home[1]], axis=1),
            jnp.concatenate([home[2], home[3]], axis=1),
        ]
    )
    return (mixer_output, attention_output)


def solution(mesh):
    ctx = ("z", "x", "core")
    split = Mesh(mesh.devices.reshape(8, 4, 2, 4), ctx + ("head",))
    rows = P(None, ctx + ("head",), None)
    in_specs = (
        rows,
        rows,
        rows,
        P(None, ctx, None),
        P(),
        P(),
        P("head"),
        P(None, "head"),
        P("head"),
        rows,
        rows,
        rows,
        P(),
    )
    out_specs = (P(None, ctx, "head"), P(None, ctx, "head"))
    return jax.shard_map(shards, mesh=split, in_specs=in_specs, out_specs=out_specs, check_vma=False)
```
